768 devices in a mesh: space: 48 (over z, y_lo, core), member: 16 (over y_hi, x).
Axes of the slice: x: 4, y: 8 (y_hi: 4, y_lo: 2; y = y_hi * 2 + y_lo), z: 12, core: 2. Of those that a mesh axis runs over, the one named last changes fastest.
Arguments:
- perturbation: float32 [16, 4, 16, 16, 6144], P('member', None, None, None, 'space'), may hold values from -6 to 6
- trajectory: bfloat16 [3, 16, 6, 16, 6144], P(None, 'member', None, None, 'space'), may hold values from -0.5 to 0.5
- site_col: int32 [48, 48, 128], P(None, 'space'), may hold values from 0 to 2047
- site_lev: int32 [48, 48, 128], P(None, 'space'), may hold values from 0 to 15
- obs_counts: int32 [48, 48], P(None, 'space'), may hold values from 0 to 128, as said below
- obs_weights: float32 [48, 48, 4, 128], P('space'), may hold values from -3 to 3
Outputs:
- final_state: float32 [16, 4, 16, 16, 6144], P('member', None, None, None, 'space')
- obs_equiv: float32 [16, 48, 48, 128], P('member', 'space')
The draws below stay inside these ranges and needn't reach their ends.
Inputs may be any that keep to these rules, and one draw needn't show every extreme that they name: obs_counts[o, s] is the number of live leading slots of owner o in tile s; some pair has exactly 128, and owners differ in load by up to four times.
All inputs are finite; a program needn't handle non-finite values.
Results may differ from the reference program's by a relative error of at most 0.0003.
Values may be sent and summed in bfloat16 or wider, within the bound.
No kernel may reach another device: no remote copies, remote signals or barrier semaphores. Data moves between devices by JAX's collectives and lax.ppermute only.
A program may use at most 64 MiB of HBM per device.

```python
import jax
import jax.numpy as jnp
from jax import lax

L = 16
LAT = 16
LOND = 128
STEPS = 3
CAP = 128
TILES = 48
LON = 6144
MEMBERS = 16


def draw_obs_counts(key, part):
    key_heavy, key_base, key_row, key_col = jax.random.split(jax.random.fold_in(key, 17), 4)
    heavy = jax.random.randint(key_heavy, (TILES, 1), 1, 5)
    base = jax.random.randint(key_base, (TILES, TILES), 0, CAP // 3 + 1)
    counts = jnp.minimum(base * heavy, CAP)
    row = jax.random.randint(key_row, (), 0, TILES)
    column = jax.random.randint(key_col, (), 0, TILES)
    return counts.at[row, column].set(CAP).astype(jnp.int32)


def with_ends(values, rng, smallest, top_value):
    longest = values.shape.index(max(values.shape))
    spots = []
    for shift in (0, 1):
        where = [jax.random.randint(jax.random.fold_in(rng, axis), (), 0, length) for axis, length in enumerate(values.shape)]
        where[longest] = (where[longest] + shift) % values.shape[longest]
        spots.append(tuple(where))
    return values.at[spots[0]].set(smallest).at[spots[1]].set(top_value)


def steps_of(rng, shape, cuts, least, top_value):
    def one(position, blocks):
        steps = jax.random.uniform(jax.random.fold_in(jax.random.fold_in(rng, 6), position), (blocks,), jnp.float32, least / len(cuts), top_value / len(cuts))
        return jnp.repeat(jnp.exp(steps), shape[position] // blocks).reshape((-1,) + (1,) * (len(shape) - position - 1))

    gain = one(*cuts[0])
    for cut in cuts[1:]:
        gain = gain * one(*cut)
    return gain


def centred(own_key, dims, spread, limit, cuts=(), kind=jnp.bfloat16):
    array = jax.random.normal(own_key, dims, jnp.float32) * spread
    if len(cuts) > 0:
        array = steps_of(own_key, dims, cuts, -0.22, 0.18) * array
    return jnp.clip(array, min=-limit, max=limit).astype(kind)


def setup_inputs(seed: int = 0) -> dict:
    keys = jax.random.split(jax.random.key(seed), 7)
    return {
        "perturbation": centred(keys[0], (MEMBERS, 4, L, LAT, LON), 1.0, 6.0, ((0, 16), (4, 48)), jnp.float32),
        "trajectory": jnp.clip(jax.random.uniform(keys[1], (STEPS, L, 6, LAT, LON), jnp.float32, -0.5, 0.5) * steps_of(keys[1], (STEPS, L, 6, LAT, LON), ((1, 16), (4, 48)), -0.4, 0.0), -0.5, 0.5).astype(jnp.bfloat16),
        "site_col": with_ends(jax.random.randint(keys[2], (TILES, TILES, CAP), 0, LAT * LOND), jax.random.fold_in(keys[2], 1), 0, (LAT * LOND) - 1).astype(jnp.int32),
        "site_lev": with_ends(jax.random.randint(keys[3], (TILES, TILES, CAP), 0, L), jax.random.fold_in(keys[3], 1), 0, L - 1).astype(jnp.int32),
        "obs_counts": draw_obs_counts(jax.random.fold_in(keys[6], 71), 0),
        "obs_weights": centred(keys[5], (TILES, TILES, 4, CAP), 0.5, 3.0, ((0, 48),), jnp.float32),
    }


def advance(state, coef):
    east = jnp.roll(state, -1, axis=-1)
    west = jnp.roll(state, 1, axis=-1)
    padded = jnp.pad(state, ((0, 0), (0, 0), (1, 1), (0, 0)))
    north = padded[:, :, 2:, :]
    south = padded[:, :, :-2, :]
    planes = coef.astype(jnp.float32)
    along = planes[:, 0][None]
    across = planes[:, 1][None]
    fresh = state - along * (east - west) * 0.5 + 0.5 * along * along * (east - 2.0 * state + west)
    fresh = fresh - across * (north - south) * 0.5 + 0.5 * across * across * (north - 2.0 * state + south)
    wind_u = state[0]
    wind_v = state[1]
    temper = fresh[2] - (planes[:, 2] * wind_u + planes[:, 3] * wind_v)
    humid = fresh[3] - (planes[:, 4] * wind_u + planes[:, 5] * wind_v)
    return jnp.stack([fresh[0], fresh[1], temper, humid], axis=0)


def reference(perturbation, trajectory, site_col, site_lev, obs_counts, obs_weights):
    def one_member(state):
        for step in range(STEPS):
            state = advance(state, trajectory[step])
        return state

    final_state = lax.map(one_member, perturbation)
    tiles = site_col.shape[1]
    lat_idx = (site_col // LOND).astype(jnp.int32)
    source = jnp.arange(tiles, dtype=jnp.int32)[None, :, None]
    lon_idx = (source * LOND + site_col % LOND).astype(jnp.int32)
    value = final_state[:, :, site_lev, lat_idx, lon_idx]
    weights = jnp.transpose(obs_weights, (2, 0, 1, 3))[None]
    summed = jnp.sum(weights * value, axis=1)
    live = jnp.arange(CAP, dtype=jnp.int32)[None, None, :] < obs_counts[:, :, None]
    obs_equiv = jnp.where(live[None], summed, jnp.float32(0.0))
    return final_state, obs_equiv
```

```python
import functools

import jax
import jax.numpy as jnp
from jax import lax
from jax.experimental import pallas as pl
from jax.experimental.pallas import tpu as pltpu
from jax.sharding import PartitionSpec as P

F32 = jnp.float32
BF16 = jnp.bfloat16
VMEM = pl.BlockSpec(memory_space=pltpu.VMEM)
HBM = pl.BlockSpec(memory_space=pltpu.HBM)


def lane_of(shape):
    return lax.broadcasted_iota(jnp.int32, shape, len(shape) - 1)


def spread_kernel(copies, t_ref, out_ref, sems):
    moves = [pltpu.make_async_copy(t_ref, out_ref.at[i], sems.at[i]) for i in range(copies)]
    for move in moves:
        move.start()
    for move in moves:
        move.wait()


def spread(planes, copies):
    return pl.pallas_call(
        functools.partial(spread_kernel, copies),
        out_shape=jax.ShapeDtypeStruct((copies,) + planes.shape, planes.dtype),
        in_specs=[VMEM],
        out_specs=HBM,
        scratch_shapes=[pltpu.SemaphoreType.DMA((copies,))],
        name="spread",
    )(planes)


def pack_kernel(levels, planes, p_ref, t_ref, out_ref):
    group = lane_of((16, 128)) // 8
    for field in range(4):
        packed = jnp.zeros((16, 128), F32)
        for level in range(levels):
            moved = pltpu.roll(p_ref[field, level], (level * 8 + 3) % 128, 1)
            packed = jnp.where(group == level, moved, packed)
        out_ref[field * 16 : field * 16 + 16, :] = packed
    packed = jnp.zeros((16, 128), F32)
    for k in range(planes):
        moved = pltpu.roll(t_ref[k * 16 : k * 16 + 16, :].astype(F32), (k * 8 + 3) % 128, 1)
        packed = jnp.where(group == k, moved, packed)
    out_ref[64:80, :] = packed


def pack_edges(state, planes):
    return pl.pallas_call(
        functools.partial(pack_kernel, 16, 12),
        out_shape=jax.ShapeDtypeStruct((80, 128), F32),
        in_specs=[VMEM, VMEM],
        out_specs=VMEM,
        name="pack_edges",
    )(state, planes)


def spread_edges_kernel(copies, west_ref, east_ref, out_ref):
    from_west = lane_of((16, 128)) % 8 < 3
    edge = jnp.where(from_west, west_ref[64:80, :], east_ref[64:80, :]).astype(BF16)
    for i in range(copies):
        out_ref[i] = edge


def spread_edges(west, east, copies):
    return pl.pallas_call(
        functools.partial(spread_edges_kernel, copies),
        out_shape=jax.ShapeDtypeStruct((copies, 16, 128), BF16),
        in_specs=[VMEM, VMEM],
        out_specs=VMEM,
        name="spread_edges",
    )(west, east)


def stencil_weights(planes):
    a, b = planes[0], planes[1]
    aa, bb = a * a, b * b
    return (
        1.0 - aa - bb,
        0.5 * (aa - a),
        0.5 * (aa + a),
        0.5 * (bb - b),
        0.5 * (bb + b),
    )


def apply_stencil(weights, planes, p, e, w, n, s):
    c0, ce, cw, cn, cs = weights
    new = [
        c0 * p[f] + ce * e[f] + cw * w[f] + cn * n[f] + cs * s[f]
        for f in range(4)
    ]
    new[2] = new[2] - (planes[2] * p[0] + planes[3] * p[1])
    new[3] = new[3] - (planes[4] * p[0] + planes[5] * p[1])
    return new


def north_south(p, first, last):
    north = [jnp.where(last, 0.0, pltpu.roll(x, 15, 0)) for x in p]
    south = [jnp.where(first, 0.0, pltpu.roll(x, 1, 0)) for x in p]
    return north, south


def advance_level(level, state, halo, t_ref, edge_planes):
    shape = (16, 128)
    lane = lane_of(shape)
    row = lax.broadcasted_iota(jnp.int32, shape, 0)
    lane_first, lane_last = lane == 0, lane == 127
    row_first, row_last = row == 0, row == 15
    for k in range(3):
        planes = [t_ref[level, (k * 6 + q) * 16 : (k * 6 + q + 1) * 16, :].astype(F32) for q in range(6)]
        east = [pltpu.roll(x, 127, 1) for x in state]
        west = [pltpu.roll(x, 1, 1) for x in state]
        halo_east = [pltpu.roll(x, 127, 1) for x in halo]
        halo_west = [pltpu.roll(x, 1, 1) for x in halo]
        north, south = north_south(state, row_first, row_last)
        new = apply_stencil(
            stencil_weights(planes),
            planes,
            state,
            [jnp.where(lane_last, h, x) for x, h in zip(east, halo_east)],
            [jnp.where(lane_first, h, x) for x, h in zip(west, halo_west)],
            north,
            south,
        )
        if k < 2:
            side = [pltpu.roll(edge_planes, (125 - (k * 6 + q) * 8) % 128, 1) for q in range(6)]
            north, south = north_south(halo, row_first, row_last)
            halo = apply_stencil(
                stencil_weights(side),
                side,
                halo,
                [jnp.where(lane_last, x, h) for x, h in zip(east, halo_east)],
                [jnp.where(lane_first, x, h) for x, h in zip(west, halo_west)],
                north,
                south,
            )
        state = new
    return state


def main_kernel(
    p_ref, t_ref, e_ref, west_ref, east_ref, row_ref, col_ref, out_ref, val_ref, halo_ref, high_ref, low_ref
):
    levels = p_ref.shape[1]
    owners = row_ref.shape[0]
    from_west = lane_of((64, 128)) % 8 < 3
    halo_ref[...] = jnp.where(from_west, west_ref[0:64, :], east_ref[0:64, :])

    def one_level(level, carry):
        shift = lax.rem(253 - level * 8, 128)
        state = [p_ref[f, level] for f in range(4)]
        halo = [pltpu.roll(halo_ref[f * 16 : f * 16 + 16, :], shift, 1) for f in range(4)]
        state = advance_level(level, state, halo, t_ref, e_ref[level].astype(F32))
        for f in range(4):
            out_ref[f, level] = state[f]
        return carry

    lax.fori_loop(0, levels, one_level, 0)

    for f in range(4):
        for half in range(2):
            block = out_ref[f, half * 8 : half * 8 + 8].reshape(128, 128)
            block = jnp.transpose(block)
            high = block.astype(BF16)
            low = (block - high.astype(F32)).astype(BF16)
            high_ref[f * 128 : f * 128 + 128, half * 128 : half * 128 + 128] = high
            low_ref[f * 128 : f * 128 + 128, half * 128 : half * 128 + 128] = low

    line = lax.broadcasted_iota(jnp.int32, (256, 128), 0)
    lon = lax.broadcasted_iota(jnp.int32, (128, 128), 0)

    def two_owners(i, carry):
        picks = []
        for o in range(2):
            hit = line == row_ref[pl.ds(2 * i + o, 1), :]
            picks.append(jnp.where(hit, 1.0, 0.0).astype(BF16))
        pick = jnp.concatenate(picks, axis=1)
        lines = jnp.dot(high_ref[...], pick, preferred_element_type=F32)
        lines = lines + jnp.dot(low_ref[...], pick, preferred_element_type=F32)
        for o in range(2):
            hit = lon == col_ref[pl.ds(2 * i + o, 1), :]
            for f in range(4):
                part = lines[f * 128 : f * 128 + 128, o * 128 : o * 128 + 128]
                val_ref[2 * i + o, f : f + 1, :] = jnp.sum(jnp.where(hit, part, 0.0), axis=0, keepdims=True)
        return carry

    lax.fori_loop(0, owners // 2, two_owners, 0)


def advance_and_pick(state, planes, edges, west, east, rows, cols):
    owners = rows.shape[0]
    return pl.pallas_call(
        main_kernel,
        out_shape=(
            jax.ShapeDtypeStruct(state.shape, F32),
            jax.ShapeDtypeStruct((owners, 4, 128), F32),
        ),
        in_specs=[VMEM] * 7,
        out_specs=(VMEM, VMEM),
        scratch_shapes=[
            pltpu.VMEM((64, 128), F32),
            pltpu.VMEM((512, 256), BF16),
            pltpu.VMEM((512, 256), BF16),
        ],
        name="advance_and_pick",
    )(state, planes, edges, west, east, rows, cols)


def on_device(perturbation, trajectory, site_col, site_lev, obs_counts, obs_weights):
    tiles, slots = site_col.shape[0], site_col.shape[2]
    members = lax.axis_size("member")
    state = perturbation[0]
    local = trajectory.reshape(288, 128)
    planes = lax.all_to_all(spread(local, members), "member", 0, 0, tiled=True)

    edges = pack_edges(state, local)
    up = [(i, (i + 1) % tiles) for i in range(tiles)]
    down = [(j, i) for i, j in up]
    west = lax.ppermute(edges, "space", up)
    east = lax.ppermute(edges, "space", down)
    side = lax.all_to_all(spread_edges(west, east, members), "member", 0, 0, tiled=True)

    live = jnp.arange(slots, dtype=jnp.int32)[None, :] < obs_counts
    rows = jnp.where(live, site_lev[:, 0, :] * 16 + site_col[:, 0, :] // 128, -1)
    cols = site_col[:, 0, :] % 128
    final, values = advance_and_pick(state, planes, side, west, east, rows, cols)
    received = lax.all_to_all(values, "space", 0, 0, tiled=True)
    summed = jnp.sum(obs_weights[0] * received, axis=1)
    return (final[None], summed.reshape(1, 1, tiles, slots))


def solution(mesh):
    in_specs = (
        P("member", None, None, None, "space"),
        P(None, "member", None, None, "space"),
        P(None, "space", None),
        P(None, "space", None),
        P(None, "space"),
        P("space", None, None, None),
    )
    out_specs = (P("member", None, None, None, "space"), P("member", "space", None, None))
    return jax.shard_map(
        on_device, mesh=mesh, in_specs=in_specs, out_specs=out_specs, check_vma=False
    )
```

```python
import functools

import jax
import jax.numpy as jnp
from jax import lax
from jax.experimental import pallas as pl
from jax.experimental.pallas import tpu as pltpu
from jax.sharding import PartitionSpec as P

F32 = jnp.float32
BF16 = jnp.bfloat16
VMEM = pl.BlockSpec(memory_space=pltpu.VMEM)
HBM = pl.BlockSpec(memory_space=pltpu.HBM)


def lane_of(shape):
    return lax.broadcasted_iota(jnp.int32, shape, len(shape) - 1)


def spread_kernel(copies, t_ref, out_ref, sems):
    rows = t_ref.shape[0]
    moves = [
        pltpu.make_async_copy(t_ref, out_ref.at[i, pl.ds(0, rows)], sems.at[i]) for i in range(copies)
    ]
    for move in moves:
        move.start()
    for move in moves:
        move.wait()


def spread(planes, copies):
    return pl.pallas_call(
        functools.partial(spread_kernel, copies),
        out_shape=jax.ShapeDtypeStruct((copies, planes.shape[0] + 16, 128), planes.dtype),
        in_specs=[VMEM],
        out_specs=HBM,
        scratch_shapes=[pltpu.SemaphoreType.DMA((copies,))],
        name="spread",
    )(planes)


def pack_state_kernel(p_ref, out_ref):
    group = lane_of((16, 128)) // 8
    for field in range(4):
        packed = jnp.zeros((16, 128), F32)
        for level in range(p_ref.shape[1]):
            moved = pltpu.roll(p_ref[field, level], (level * 8 + 3) % 128, 1)
            packed = jnp.where(group == level, moved, packed)
        out_ref[field * 16 : field * 16 + 16, :] = packed


def pack_state(state):
    return pl.pallas_call(
        pack_state_kernel,
        out_shape=jax.ShapeDtypeStruct((64, 128), F32),
        in_specs=[VMEM],
        out_specs=VMEM,
        name="pack_state",
    )(state)


def pack_planes_kernel(t_ref, out_ref):
    group = lane_of((16, 128)) // 8
    packed = jnp.zeros((16, 128), F32)
    for k in range(12):
        moved = pltpu.roll(t_ref[k * 16 : k * 16 + 16, :].astype(F32), (k * 8 + 3) % 128, 1)
        packed = jnp.where(group == k, moved, packed)
    out_ref[...] = packed.astype(BF16)


def pack_planes(planes):
    return pl.pallas_call(
        pack_planes_kernel,
        out_shape=jax.ShapeDtypeStruct((16, 128), BF16),
        in_specs=[VMEM],
        out_specs=VMEM,
        name="pack_planes",
    )(planes)


def from_partner(shape, odd):
    return (lane_of(shape) % 8 < 3) == (odd == 1)


def fill_kernel(odd_ref, near_ref, far_ref, whole_ref, out_ref, edge_ref, sem):
    near, far = near_ref[...].astype(F32), far_ref[...].astype(F32)
    edge = jnp.where(from_partner((16, 128), odd_ref[0]), near, far).astype(BF16)
    for i in range(edge_ref.shape[0]):
        edge_ref[i] = edge
    rows = out_ref.shape[1] - 16
    move = pltpu.make_async_copy(edge_ref, out_ref.at[:, pl.ds(rows, 16)], sem)
    move.start()
    move.wait()


def fill_edges(odd, near, far, whole):
    return pl.pallas_call(
        fill_kernel,
        out_shape=jax.ShapeDtypeStruct(whole.shape, whole.dtype),
        in_specs=[pl.BlockSpec(memory_space=pltpu.SMEM), VMEM, VMEM, HBM],
        out_specs=HBM,
        scratch_shapes=[pltpu.VMEM((whole.shape[0], 16, 128), BF16), pltpu.SemaphoreType.DMA],
        input_output_aliases={3: 0},
        name="fill_edges",
    )(odd, near, far, whole)


def stencil_weights(planes):
    a, b = planes[0], planes[1]
    aa, bb = a * a, b * b
    return (
        1.0 - aa - bb,
        0.5 * (aa - a),
        0.5 * (aa + a),
        0.5 * (bb - b),
        0.5 * (bb + b),
    )


def apply_stencil(weights, planes, p, e, w, n, s):
    c0, ce, cw, cn, cs = weights
    new = [
        c0 * p[f] + ce * e[f] + cw * w[f] + cn * n[f] + cs * s[f]
        for f in range(4)
    ]
    new[2] = new[2] - (planes[2] * p[0] + planes[3] * p[1])
    new[3] = new[3] - (planes[4] * p[0] + planes[5] * p[1])
    return new


def north_south(p, first, last):
    north = [jnp.where(last, 0.0, pltpu.roll(x, 15, 0)) for x in p]
    south = [jnp.where(first, 0.0, pltpu.roll(x, 1, 0)) for x in p]
    return north, south


def advance_level(level, state, halo, t_ref, edge_planes):
    shape = (16, 128)
    lane = lane_of(shape)
    row = lax.broadcasted_iota(jnp.int32, shape, 0)
    lane_first, lane_last = lane == 0, lane == 127
    row_first, row_last = row == 0, row == 15
    for k in range(3):
        planes = [t_ref[level, (k * 6 + q) * 16 : (k * 6 + q + 1) * 16, :].astype(F32) for q in range(6)]
        east = [pltpu.roll(x, 127, 1) for x in state]
        west = [pltpu.roll(x, 1, 1) for x in state]
        halo_east = [pltpu.roll(x, 127, 1) for x in halo]
        halo_west = [pltpu.roll(x, 1, 1) for x in halo]
        north, south = north_south(state, row_first, row_last)
        new = apply_stencil(
            stencil_weights(planes),
            planes,
            state,
            [jnp.where(lane_last, h, x) for x, h in zip(east, halo_east)],
            [jnp.where(lane_first, h, x) for x, h in zip(west, halo_west)],
            north,
            south,
        )
        if k < 2:
            side = [pltpu.roll(edge_planes, (125 - (k * 6 + q) * 8) % 128, 1) for q in range(6)]
            north, south = north_south(halo, row_first, row_last)
            halo = apply_stencil(
                stencil_weights(side),
                side,
                halo,
                [jnp.where(lane_last, x, h) for x, h in zip(east, halo_east)],
                [jnp.where(lane_first, x, h) for x, h in zip(west, halo_west)],
                north,
                south,
            )
        state = new
    return state


def main_kernel(
    odd_ref, p_ref, t_ref, near_ref, far_ref, row_ref, col_ref, out_ref, val_ref, halo_ref, high_ref, low_ref
):
    levels = p_ref.shape[1]
    owners = row_ref.shape[0]
    halo_ref[...] = jnp.where(from_partner((64, 128), odd_ref[0]), near_ref[...], far_ref[...])

    def one_level(level, carry):
        shift = lax.rem(253 - level * 8, 128)
        state = [p_ref[f, level] for f in range(4)]
        halo = [pltpu.roll(halo_ref[f * 16 : f * 16 + 16, :], shift, 1) for f in range(4)]
        state = advance_level(level, state, halo, t_ref, t_ref[level, 288:304, :].astype(F32))
        for f in range(4):
            out_ref[f, level] = state[f]
        return carry

    lax.fori_loop(0, levels, one_level, 0, unroll=2)

    for f in range(4):
        for half in range(2):
            block = out_ref[f, half * 8 : half * 8 + 8].reshape(128, 128)
            block = jnp.transpose(block)
            high = block.astype(BF16)
            low = (block - high.astype(F32)).astype(BF16)
            high_ref[f * 128 : f * 128 + 128, half * 128 : half * 128 + 128] = high
            low_ref[f * 128 : f * 128 + 128, half * 128 : half * 128 + 128] = low

    line = lax.broadcasted_iota(jnp.int32, (256, 128), 0)
    lon = lax.broadcasted_iota(jnp.int32, (128, 128), 0)

    def two_owners(i, carry):
        picks = []
        for o in range(2):
            hit = line == row_ref[pl.ds(2 * i + o, 1), :]
            picks.append(jnp.where(hit, 1.0, 0.0).astype(BF16))
        pick = jnp.concatenate(picks, axis=1)
        lines = jnp.dot(high_ref[...], pick, preferred_element_type=F32)
        lines = lines + jnp.dot(low_ref[...], pick, preferred_element_type=F32)
        for o in range(2):
            hit = lon == col_ref[pl.ds(2 * i + o, 1), :]
            for f in range(4):
                part = lines[f * 128 : f * 128 + 128, o * 128 : o * 128 + 128]
                val_ref[2 * i + o, f : f + 1, :] = jnp.sum(jnp.where(hit, part, 0.0), axis=0, keepdims=True)
        return carry

    lax.fori_loop(0, owners // 2, two_owners, 0, unroll=2)


def advance_and_pick(odd, state, planes, near, far, rows, cols):
    owners = rows.shape[0]
    return pl.pallas_call(
        main_kernel,
        out_shape=(
            jax.ShapeDtypeStruct(state.shape, F32),
            jax.ShapeDtypeStruct((owners, 4, 128), F32),
        ),
        in_specs=[pl.BlockSpec(memory_space=pltpu.SMEM)] + [VMEM] * 6,
        out_specs=(VMEM, VMEM),
        scratch_shapes=[
            pltpu.VMEM((64, 128), F32),
            pltpu.VMEM((512, 256), BF16),
            pltpu.VMEM((512, 256), BF16),
        ],
        name="advance_and_pick",
    )(odd, state, planes, near, far, rows, cols)


def on_device(perturbation, trajectory, site_col, site_lev, obs_counts, obs_weights):
    tiles, slots = site_col.shape[0], site_col.shape[2]
    members = lax.axis_size("member")
    state = perturbation[0]
    local = trajectory.reshape(288, 128)
    odd = (lax.axis_index("space") % 2).astype(jnp.int32).reshape(1)
    pairs = [(i, i ^ 1) for i in range(tiles)]
    crossed = [(i, (i + 1) % tiles if i % 2 else (i - 1) % tiles) for i in range(tiles)]

    edge = pack_planes(local)
    far = lax.ppermute(edge, "space", crossed)
    near = lax.ppermute(edge, "space", pairs)
    copies = fill_edges(odd, near, far, spread(local, members))
    planes = lax.all_to_all(copies, "member", 0, 0, tiled=True)

    state_late, _ = lax.optimization_barrier((state, copies))
    edge = pack_state(state_late)
    far = lax.ppermute(edge, "space", crossed)
    near = lax.ppermute(edge, "space", pairs)

    live = jnp.arange(slots, dtype=jnp.int32)[None, :] < obs_counts
    rows = jnp.where(live, site_lev[:, 0, :] * 16 + site_col[:, 0, :] // 128, -1)
    cols = site_col[:, 0, :] % 128
    planes = pltpu.with_memory_space_constraint(planes, pltpu.VMEM)
    near = pltpu.with_memory_space_constraint(near, pltpu.VMEM)
    far = pltpu.with_memory_space_constraint(far, pltpu.VMEM)
    final, values = advance_and_pick(odd, state, planes, near, far, rows, cols)
    received = lax.all_to_all(values, "space", 0, 0, tiled=True)
    summed = jnp.sum(obs_weights[0] * received, axis=1)
    return (final[None], summed.reshape(1, 1, tiles, slots))


def solution(mesh):
    in_specs = (
        P("member", None, None, None, "space"),
        P(None, "member", None, None, "space"),
        P(None, "space", None),
        P(None, "space", None),
        P(None, "space"),
        P("space", None, None, None),
    )
    out_specs = (P("member", None, None, None, "space"), P("member", "space", None, None))
    return jax.shard_map(
        on_device, mesh=mesh, in_specs=in_specs, out_specs=out_specs, check_vma=False
    )
```

```python
import functools

import jax
import jax.numpy as jnp
import numpy as np
from jax import lax
from jax.experimental import pallas as pl
from jax.experimental.pallas import tpu as pltpu
from jax.sharding import Mesh
from jax.sharding import PartitionSpec as P

F32 = jnp.float32
BF16 = jnp.bfloat16
VMEM = pl.BlockSpec(memory_space=pltpu.VMEM)
SMEM = pl.BlockSpec(memory_space=pltpu.SMEM)
HBM = pl.BlockSpec(memory_space=pltpu.HBM)
TILE = (16, 128)


def lane_of(shape):
    return lax.broadcasted_iota(jnp.int32, shape, len(shape) - 1)


def pack_kernel(pos_ref, p_ref, t_ref, edge_ref, copies_ref, s1_ref, s2_ref, s3_ref, copy_sems, send_sems):
    x = pos_ref[1]
    moves = []
    for i in range(copies_ref.shape[0]):
        moves.append(pltpu.make_async_copy(t_ref, copies_ref.at[i, pl.ds(0, 288)], copy_sems.at[i]))
    for k, send in enumerate((s1_ref, s2_ref, s3_ref)):
        peer = lax.rem(x + k + 1, 4)
        for f in range(4):
            moves.append(
                pltpu.make_async_copy(p_ref.at[f, :, peer], send.at[pl.ds(4 * f, 4)], send_sems.at[k, f])
            )
    for move in moves:
        move.start()
    group = lane_of(TILE) // 8
    for x_of in range(4):
        packed = jnp.zeros(TILE, F32)
        for g in range(16):
            moved = pltpu.roll(p_ref[g // 4, g % 4, x_of], (g * 8 + 3) % 128, 1)
            packed = jnp.where(group == g, moved, packed)
        edge_ref[x_of * 16 : x_of * 16 + 16, :] = packed
    packed = jnp.zeros(TILE, F32)
    for k in range(12):
        moved = pltpu.roll(t_ref[k * 16 : k * 16 + 16, :].astype(F32), (k * 8 + 3) % 128, 1)
        packed = jnp.where(group == k, moved, packed)
    edge_ref[64:80, :] = packed
    for move in moves:
        move.wait()


def pack(pos, state, planes):
    send = jax.ShapeDtypeStruct((17,) + TILE, F32)
    return pl.pallas_call(
        pack_kernel,
        out_shape=(
            jax.ShapeDtypeStruct((80, 128), F32),
            jax.ShapeDtypeStruct((4, 304, 128), BF16),
            send,
            send,
            send,
        ),
        in_specs=[SMEM, VMEM, VMEM],
        out_specs=(VMEM, HBM, HBM, HBM, HBM),
        scratch_shapes=[pltpu.SemaphoreType.DMA((4,)), pltpu.SemaphoreType.DMA((3, 4))],
        name="pack",
    )(pos, state, planes)


def fill_kernel(
    pos_ref, near_ref, far_ref, c_in, s1_in, s2_in, s3_in, own_ref, c_ref, s1_ref, s2_ref, s3_ref, all_ref, side_ref, sems
):
    odd, x = pos_ref[0], pos_ref[1]
    from_near = (lane_of((80, 128)) % 8 < 3) == (odd == 1)
    edge = jnp.where(from_near, near_ref[...], far_ref[...])
    for i in range(4):
        all_ref[i] = edge[i * 16 : i * 16 + 16]
        side_ref[i] = edge[64:80].astype(BF16)
    moves = [pltpu.make_async_copy(side_ref, c_ref.at[:, pl.ds(288, 16)], sems.at[0])]
    for k, send in enumerate((s1_ref, s2_ref, s3_ref)):
        moves.append(pltpu.make_async_copy(all_ref.at[lax.rem(x + k + 1, 4)], send.at[16], sems.at[k + 1]))
    for move in moves:
        move.start()
    own_ref[...] = all_ref[x]
    for move in moves:
        move.wait()


def fill(pos, near, far, copies, sends):
    send = jax.ShapeDtypeStruct((17,) + TILE, F32)
    near = pltpu.with_memory_space_constraint(near, pltpu.VMEM)
    far = pltpu.with_memory_space_constraint(far, pltpu.VMEM)
    return pl.pallas_call(
        fill_kernel,
        out_shape=(jax.ShapeDtypeStruct(TILE, F32), jax.ShapeDtypeStruct(copies.shape, BF16), send, send, send),
        in_specs=[SMEM, VMEM, VMEM, HBM, HBM, HBM, HBM],
        out_specs=(VMEM, HBM, HBM, HBM, HBM),
        scratch_shapes=[
            pltpu.VMEM((4,) + TILE, F32),
            pltpu.VMEM((4,) + TILE, BF16),
            pltpu.SemaphoreType.DMA((4,)),
        ],
        input_output_aliases={3: 1, 4: 2, 5: 3, 6: 4},
        name="fill",
    )(pos, near, far, copies, *sends)


def weights_of(planes, first, last):
    a, b = planes[0], planes[1]
    aa, bb = a * a, b * b
    return [
        1.0 - aa - bb,
        0.5 * (aa - a),
        0.5 * (aa + a),
        jnp.where(last, 0.0, 0.5 * (bb - b)),
        jnp.where(first, 0.0, 0.5 * (bb + b)),
    ] + planes[2:]


def apply_stencil(w_ref, k, p, east, west):
    new = []
    for f in range(4):
        north, south = pltpu.roll(p[f], 15, 0), pltpu.roll(p[f], 1, 0)
        new.append(
            (w_ref[k, 0] * p[f] + w_ref[k, 1] * east[f])
            + (w_ref[k, 2] * west[f] + (w_ref[k, 3] * north + w_ref[k, 4] * south))
        )
    new[2] = new[2] - (w_ref[k, 5] * p[0] + w_ref[k, 6] * p[1])
    new[3] = new[3] - (w_ref[k, 7] * p[0] + w_ref[k, 8] * p[1])
    return new


def advance_kernel(pos_ref, p_ref, own_ref, r1_ref, r2_ref, r3_ref, t_ref, out_ref, w_ref, h_ref):
    x = pos_ref[1]
    lane = lane_of(TILE)
    row = lax.broadcasted_iota(jnp.int32, TILE, 0)
    lane_first, lane_last = lane == 0, lane == 127
    row_first, row_last = row == 0, row == 15

    def one_level(y, carry):
        side = t_ref[y, 288:304, :].astype(F32)
        for k in range(3):
            planes = [t_ref[y, (k * 6 + q) * 16 : (k * 6 + q + 1) * 16, :].astype(F32) for q in range(6)]
            for i, weight in enumerate(weights_of(planes, row_first, row_last)):
                w_ref[k, i] = weight
            if k < 2:
                planes = [pltpu.roll(side, (125 - (k * 6 + q) * 8) % 128, 1) for q in range(6)]
                for i, weight in enumerate(weights_of(planes, row_first, row_last)):
                    h_ref[k, i] = weight
        for m, source in enumerate((None, r1_ref, r2_ref, r3_ref)):
            if source is None:
                state = [p_ref[f, y, x] for f in range(4)]
                edge = own_ref[...]
            else:
                state = [source[4 * f + y] for f in range(4)]
                edge = source[16]
            halo = [pltpu.roll(edge, lax.rem(253 - (4 * f + y) * 8, 128), 1) for f in range(4)]
            for k in range(3):
                east = [pltpu.roll(v, 127, 1) for v in state]
                west = [pltpu.roll(v, 1, 1) for v in state]
                halo_east = [pltpu.roll(v, 127, 1) for v in halo]
                halo_west = [pltpu.roll(v, 1, 1) for v in halo]
                new = apply_stencil(
                    w_ref,
                    k,
                    state,
                    [jnp.where(lane_last, h, v) for v, h in zip(east, halo_east)],
                    [jnp.where(lane_first, h, v) for v, h in zip(west, halo_west)],
                )
                if k < 2:
                    halo = apply_stencil(
                        h_ref,
                        k,
                        halo,
                        [jnp.where(lane_last, v, h) for v, h in zip(east, halo_east)],
                        [jnp.where(lane_first, v, h) for v, h in zip(west, halo_west)],
                    )
                state = new
            for f in range(4):
                out_ref[lax.rem(x + 4 - m, 4), f, y] = state[f]
        return carry

    lax.fori_loop(0, 4, one_level, 0)


def advance(pos, state, own, received, planes):
    received = [pltpu.with_memory_space_constraint(r, pltpu.VMEM) for r in received]
    planes = pltpu.with_memory_space_constraint(planes, pltpu.VMEM)
    return pl.pallas_call(
        advance_kernel,
        out_shape=jax.ShapeDtypeStruct((4, 4, 4) + TILE, F32),
        in_specs=[SMEM] + [VMEM] * 6,
        out_specs=VMEM,
        scratch_shapes=[pltpu.VMEM((3, 9) + TILE, F32), pltpu.VMEM((2, 9) + TILE, F32)],
        name="advance",
    )(pos, state, own, *received, planes)


def pick_kernel(b_ref, row_ref, col_ref, out_ref, val_ref, high_ref, low_ref, sems):
    owners = row_ref.shape[0]
    moves = [pltpu.make_async_copy(b_ref.at[x], out_ref.at[:, :, x], sems.at[x]) for x in range(4)]
    for move in moves:
        move.start()
    for f in range(4):
        for half in range(2):
            block = jnp.concatenate(
                [b_ref[2 * half, f].reshape(64, 128), b_ref[2 * half + 1, f].reshape(64, 128)], axis=0
            )
            block = jnp.transpose(block)
            high = block.astype(BF16)
            low = (block - high.astype(F32)).astype(BF16)
            high_ref[f * 128 : f * 128 + 128, half * 128 : half * 128 + 128] = high
            low_ref[f * 128 : f * 128 + 128, half * 128 : half * 128 + 128] = low

    line = lax.broadcasted_iota(jnp.int32, (256, 128), 0)
    lon = lax.broadcasted_iota(jnp.int32, (128, 128), 0)

    def two_owners(i, carry):
        picks = []
        for o in range(2):
            hit = line == row_ref[pl.ds(2 * i + o, 1), :]
            picks.append(jnp.where(hit, 1.0, 0.0).astype(BF16))
        pick = jnp.concatenate(picks, axis=1)
        lines = jnp.dot(high_ref[...], pick, preferred_element_type=F32)
        lines = lines + jnp.dot(low_ref[...], pick, preferred_element_type=F32)
        for o in range(2):
            hit = lon == col_ref[pl.ds(2 * i + o, 1), :]
            for f in range(4):
                part = lines[f * 128 : f * 128 + 128, o * 128 : o * 128 + 128]
                val_ref[2 * i + o, f : f + 1, :] = jnp.sum(jnp.where(hit, part, 0.0), axis=0, keepdims=True)
        return carry

    lax.fori_loop(0, owners // 2, two_owners, 0, unroll=2)
    for move in moves:
        move.wait()


def pick(blocks, rows, cols):
    owners = rows.shape[0]
    blocks = pltpu.with_memory_space_constraint(blocks, pltpu.VMEM)
    return pl.pallas_call(
        pick_kernel,
        out_shape=(
            jax.ShapeDtypeStruct((4, 4, 4) + TILE, F32),
            jax.ShapeDtypeStruct((owners, 4, 128), F32),
        ),
        in_specs=[VMEM] * 3,
        out_specs=(HBM, VMEM),
        scratch_shapes=[
            pltpu.VMEM((512, 256), BF16),
            pltpu.VMEM((512, 256), BF16),
            pltpu.SemaphoreType.DMA((4,)),
        ],
        name="pick",
    )(blocks, rows, cols)


def on_device(perturbation, trajectory, site_col, site_lev, obs_counts, obs_weights):
    tiles, slots = site_col.shape[0], site_col.shape[2]
    state = perturbation.reshape((4, 4, 4) + TILE)
    local = trajectory.reshape(288, 128)
    pos = jnp.stack([lax.axis_index("space") % 2, lax.axis_index("x")]).astype(jnp.int32)
    pairs = [(i, i ^ 1) for i in range(tiles)]
    crossed = [(i, (i + 1) % tiles if i % 2 else (i - 1) % tiles) for i in range(tiles)]

    edge, copies, *sends = pack(pos, state, local)
    far = lax.ppermute(edge, "space", crossed)
    near = lax.ppermute(edge, "space", pairs)
    own, copies, *sends = fill(pos, near, far, copies, sends)
    planes = lax.all_to_all(copies, "yhi", 0, 0, tiled=True)
    received = [
        lax.ppermute(send, "x", [(i, (i + k + 1) % 4) for i in range(4)]) for k, send in enumerate(sends)
    ]
    blocks = advance(pos, state, own, received, planes)
    blocks = lax.all_to_all(blocks, "x", 0, 0, tiled=True)

    live = jnp.arange(slots, dtype=jnp.int32)[None, :] < obs_counts
    level, col = site_lev[:, 0, :], site_col[:, 0, :]
    rows = jnp.where(live, (level % 4) * 64 + (level // 4) * 16 + col // 128, -1)
    final, values = pick(blocks, rows, col % 128)
    received = lax.all_to_all(values, "space", 0, 0, tiled=True)
    summed = jnp.sum(obs_weights[0] * received, axis=1)
    return (final.reshape(perturbation.shape), summed.reshape(1, 1, tiles, slots))


def solution(mesh):
    member = ("yhi", "x")
    fine = Mesh(np.asarray(mesh.devices).reshape(mesh.shape["space"], 4, 4), ("space",) + member)
    in_specs = (
        P(member, None, None, None, "space"),
        P(None, member, None, None, "space"),
        P(None, "space", None),
        P(None, "space", None),
        P(None, "space"),
        P("space", None, None, None),
    )
    out_specs = (P(member, None, None, None, "space"), P(member, "space", None, None))
    return jax.shard_map(
        on_device, mesh=fine, in_specs=in_specs, out_specs=out_specs, check_vma=False
    )
```

```python
import functools

import jax
import jax.numpy as jnp
import numpy as np
from jax import lax
from jax.experimental import pallas as pl
from jax.experimental.pallas import tpu as pltpu
from jax.sharding import Mesh
from jax.sharding import PartitionSpec as P

F32 = jnp.float32
BF16 = jnp.bfloat16
VMEM = pl.BlockSpec(memory_space=pltpu.VMEM)
HBM = pl.BlockSpec(memory_space=pltpu.HBM)
TILE = (16, 128)


axis_index = lax.axis_index


def lane_of(shape):
    return lax.broadcasted_iota(jnp.int32, shape, len(shape) - 1)


def send_kernel(p_ref, t_ref, blocks_ref, copies_ref, edge_ref, block_sems, copy_sems):
    moves = [pltpu.make_async_copy(p_ref.at[:, :, x], blocks_ref.at[x], block_sems.at[x]) for x in range(4)]
    moves += [
        pltpu.make_async_copy(t_ref, copies_ref.at[i, pl.ds(0, 288)], copy_sems.at[i]) for i in range(4)
    ]
    for move in moves:
        move.start()
    group = lane_of(TILE) // 8
    packed = jnp.zeros(TILE, F32)
    for k in range(12):
        moved = pltpu.roll(t_ref[k * 16 : k * 16 + 16, :].astype(F32), (k * 8 + 3) % 128, 1)
        packed = jnp.where(group == k, moved, packed)
    edge_ref[...] = packed.astype(BF16)
    for move in moves:
        move.wait()


def send(state, planes):
    return pl.pallas_call(
        send_kernel,
        out_shape=(
            jax.ShapeDtypeStruct((4, 4, 4) + TILE, F32),
            jax.ShapeDtypeStruct((4, 304, 128), BF16),
            jax.ShapeDtypeStruct(TILE, BF16),
        ),
        in_specs=[HBM, VMEM],
        out_specs=(HBM, HBM, VMEM),
        scratch_shapes=[pltpu.SemaphoreType.DMA((4,)), pltpu.SemaphoreType.DMA((4,))],
        name="send",
    )(state, planes)


def merge(near, far):
    odd = axis_index("space") % 2
    return jnp.where((lane_of(near.shape) % 8 < 3) == (odd == 1), near, far)


def fill_kernel(near_ref, far_ref, c_in, c_ref, side_ref, sem):
    edge = merge(near_ref[...].astype(F32), far_ref[...].astype(F32)).astype(BF16)
    for i in range(4):
        side_ref[i] = edge
    move = pltpu.make_async_copy(side_ref, c_ref.at[:, pl.ds(288, 16)], sem)
    move.start()
    move.wait()


def in_vmem(x):
    return pltpu.with_memory_space_constraint(x, pltpu.VMEM)


def fill(near, far, copies):
    return pl.pallas_call(
        fill_kernel,
        out_shape=jax.ShapeDtypeStruct(copies.shape, BF16),
        in_specs=[VMEM, VMEM, HBM],
        out_specs=HBM,
        scratch_shapes=[pltpu.VMEM((4,) + TILE, BF16), pltpu.SemaphoreType.DMA],
        input_output_aliases={2: 0},
        name="fill",
    )(in_vmem(near), in_vmem(far), copies)


def pack_kernel(p_ref, edge_ref):
    group = lane_of(TILE) // 8
    for m in range(4):
        packed = jnp.zeros(TILE, F32)
        for g in range(16):
            moved = pltpu.roll(p_ref[m, g // 4, g % 4], (g * 8 + 3) % 128, 1)
            packed = jnp.where(group == g, moved, packed)
        edge_ref[m] = packed


def pack(states):
    return pl.pallas_call(
        pack_kernel,
        out_shape=jax.ShapeDtypeStruct((4,) + TILE, F32),
        in_specs=[VMEM],
        out_specs=VMEM,
        name="pack",
    )(in_vmem(states))


def weights_of(planes, first, last):
    a, b = planes[0], planes[1]
    aa, bb = a * a, b * b
    return [
        1.0 - aa - bb,
        0.5 * (aa - a),
        0.5 * (aa + a),
        jnp.where(last, 0.0, 0.5 * (bb - b)),
        jnp.where(first, 0.0, 0.5 * (bb + b)),
    ] + planes[2:]


def apply_stencil(w_ref, k, p, east, west):
    new = []
    for f in range(4):
        north, south = pltpu.roll(p[f], 15, 0), pltpu.roll(p[f], 1, 0)
        new.append(
            (w_ref[k, 0] * p[f] + w_ref[k, 1] * east[f])
            + (w_ref[k, 2] * west[f] + (w_ref[k, 3] * north + w_ref[k, 4] * south))
        )
    new[2] = new[2] - (w_ref[k, 5] * p[0] + w_ref[k, 6] * p[1])
    new[3] = new[3] - (w_ref[k, 7] * p[0] + w_ref[k, 8] * p[1])
    return new


def advance_kernel(p_ref, near_ref, far_ref, t_ref, out_ref, w_ref, h_ref, edge_ref):
    lane = lane_of(TILE)
    row = lax.broadcasted_iota(jnp.int32, TILE, 0)
    lane_first, lane_last = lane == 0, lane == 127
    row_first, row_last = row == 0, row == 15
    edge_ref[...] = merge(near_ref[...], far_ref[...])

    def one_level(y, carry):
        side = t_ref[y, 288:304, :].astype(F32)
        for k in range(3):
            planes = [t_ref[y, (k * 6 + q) * 16 : (k * 6 + q + 1) * 16, :].astype(F32) for q in range(6)]
            for i, weight in enumerate(weights_of(planes, row_first, row_last)):
                w_ref[k, i] = weight
            if k < 2:
                planes = [pltpu.roll(side, (125 - (k * 6 + q) * 8) % 128, 1) for q in range(6)]
                for i, weight in enumerate(weights_of(planes, row_first, row_last)):
                    h_ref[k, i] = weight
        for m in range(4):
            state = [p_ref[m, f, y] for f in range(4)]
            edge = edge_ref[m]
            halo = [pltpu.roll(edge, lax.rem(253 - (4 * f + y) * 8, 128), 1) for f in range(4)]
            for k in range(3):
                east = [pltpu.roll(v, 127, 1) for v in state]
                west = [pltpu.roll(v, 1, 1) for v in state]
                halo_east = [pltpu.roll(v, 127, 1) for v in halo]
                halo_west = [pltpu.roll(v, 1, 1) for v in halo]
                new = apply_stencil(
                    w_ref,
                    k,
                    state,
                    [jnp.where(lane_last, h, v) for v, h in zip(east, halo_east)],
                    [jnp.where(lane_first, h, v) for v, h in zip(west, halo_west)],
                )
                if k < 2:
                    halo = apply_stencil(
                        h_ref,
                        k,
                        halo,
                        [jnp.where(lane_last, v, h) for v, h in zip(east, halo_east)],
                        [jnp.where(lane_first, v, h) for v, h in zip(west, halo_west)],
                    )
                state = new
            for f in range(4):
                out_ref[m, f, y] = state[f]
        return carry

    lax.fori_loop(0, 4, one_level, 0)


def advance(states, near, far, planes):
    return pl.pallas_call(
        advance_kernel,
        out_shape=pltpu.VMEM((4, 4, 4) + TILE, F32),
        in_specs=[VMEM] * 4,
        out_specs=VMEM,
        scratch_shapes=[
            pltpu.VMEM((3, 9) + TILE, F32),
            pltpu.VMEM((2, 9) + TILE, F32),
            pltpu.VMEM((4,) + TILE, F32),
        ],
        name="advance",
    )(in_vmem(states), in_vmem(near), in_vmem(far), in_vmem(planes))


def pick_kernel(b_ref, row_ref, col_ref, out_ref, val_ref, high_ref, low_ref, sems):
    owners = row_ref.shape[0]
    moves = [pltpu.make_async_copy(b_ref.at[x], out_ref.at[:, :, x], sems.at[x]) for x in range(4)]
    for move in moves:
        move.start()
    for f in range(4):
        for half in range(2):
            block = jnp.concatenate(
                [b_ref[2 * half, f].reshape(64, 128), b_ref[2 * half + 1, f].reshape(64, 128)], axis=0
            )
            block = jnp.transpose(block)
            high = block.astype(BF16)
            low = (block - high.astype(F32)).astype(BF16)
            high_ref[f * 128 : f * 128 + 128, half * 128 : half * 128 + 128] = high
            low_ref[f * 128 : f * 128 + 128, half * 128 : half * 128 + 128] = low

    line = lax.broadcasted_iota(jnp.int32, (256, 128), 0)
    lon = lax.broadcasted_iota(jnp.int32, (128, 128), 0)

    def two_owners(i, carry):
        picks = []
        for o in range(2):
            hit = line == row_ref[pl.ds(2 * i + o, 1), :]
            picks.append(jnp.where(hit, 1.0, 0.0).astype(BF16))
        pick = jnp.concatenate(picks, axis=1)
        lines = jnp.dot(high_ref[...], pick, preferred_element_type=F32)
        lines = lines + jnp.dot(low_ref[...], pick, preferred_element_type=F32)
        for o in range(2):
            hit = lon == col_ref[pl.ds(2 * i + o, 1), :]
            for f in range(4):
                part = lines[f * 128 : f * 128 + 128, o * 128 : o * 128 + 128]
                val_ref[2 * i + o, f : f + 1, :] = jnp.sum(jnp.where(hit, part, 0.0), axis=0, keepdims=True)
        return carry

    lax.fori_loop(0, owners // 2, two_owners, 0, unroll=2)
    for move in moves:
        move.wait()


def pick(blocks, rows, cols):
    owners = rows.shape[0]
    return pl.pallas_call(
        pick_kernel,
        out_shape=(
            jax.ShapeDtypeStruct((4, 4, 4) + TILE, F32),
            jax.ShapeDtypeStruct((owners, 4, 128), F32),
        ),
        in_specs=[VMEM] * 3,
        out_specs=(HBM, VMEM),
        scratch_shapes=[
            pltpu.VMEM((512, 256), BF16),
            pltpu.VMEM((512, 256), BF16),
            pltpu.SemaphoreType.DMA((4,)),
        ],
        name="pick",
    )(in_vmem(blocks), rows, cols)


def on_device(perturbation, trajectory, site_col, site_lev, obs_counts, obs_weights):
    tiles, slots = site_col.shape[0], site_col.shape[2]
    state = perturbation.reshape((4, 4, 4) + TILE)
    local = trajectory.reshape(288, 128)
    pairs = [(i, i ^ 1) for i in range(tiles)]
    crossed = [(i, (i + 1) % tiles if i % 2 else (i - 1) % tiles) for i in range(tiles)]

    blocks, copies, edge = send(state, local)
    states = lax.all_to_all(blocks, "x", 0, 0, tiled=True)
    far = lax.ppermute(edge, "space", crossed)
    near = lax.ppermute(edge, "space", pairs)
    copies = fill(near, far, copies)
    planes = lax.all_to_all(copies, "yhi", 0, 0, tiled=True)

    late, _ = lax.optimization_barrier((states, copies))
    edge = pack(late)
    far = lax.ppermute(edge, "space", crossed)
    near = lax.ppermute(edge, "space", pairs)
    blocks = advance(states, near, far, planes)
    blocks = lax.all_to_all(blocks, "x", 0, 0, tiled=True)

    live = jnp.arange(slots, dtype=jnp.int32)[None, :] < obs_counts
    level, col = site_lev[:, 0, :], site_col[:, 0, :]
    rows = jnp.where(live, (level % 4) * 64 + (level // 4) * 16 + col // 128, -1)
    final, values = pick(blocks, rows, col % 128)
    received = lax.all_to_all(values, "space", 0, 0, tiled=True)
    summed = jnp.sum(obs_weights[0] * received, axis=1)
    return (final.reshape(perturbation.shape), summed.reshape(1, 1, tiles, slots))


def solution(mesh):
    member = ("yhi", "x")
    fine = Mesh(np.asarray(mesh.devices).reshape(mesh.shape["space"], 4, 4), ("space",) + member)
    in_specs = (
        P(member, None, None, None, "space"),
        P(None, member, None, None, "space"),
        P(None, "space", None),
        P(None, "space", None),
        P(None, "space"),
        P("space", None, None, None),
    )
    out_specs = (P(member, None, None, None, "space"), P(member, "space", None, None))
    return jax.shard_map(
        on_device, mesh=fine, in_specs=in_specs, out_specs=out_specs, check_vma=False
    )
```

```python
import functools

import jax
import jax.numpy as jnp
import numpy as np
from jax import lax
from jax.experimental import pallas as pl
from jax.experimental.pallas import tpu as pltpu
from jax.sharding import Mesh
from jax.sharding import PartitionSpec as P

F32 = jnp.float32
BF16 = jnp.bfloat16
VMEM = pl.BlockSpec(memory_space=pltpu.VMEM)
HBM = pl.BlockSpec(memory_space=pltpu.HBM)
TILE = (16, 128)


axis_index = lax.axis_index


def lane_of(shape):
    return lax.broadcasted_iota(jnp.int32, shape, len(shape) - 1)


def send_kernel(p_ref, t_ref, blocks_ref, copies_ref, edge_ref, block_sems, copy_sems):
    moves = [pltpu.make_async_copy(p_ref.at[:, :, x], blocks_ref.at[x], block_sems.at[x]) for x in range(4)]
    moves += [
        pltpu.make_async_copy(t_ref, copies_ref.at[i, pl.ds(0, 288)], copy_sems.at[i]) for i in range(4)
    ]
    for move in moves:
        move.start()
    group = lane_of(TILE) // 8
    packed = jnp.zeros(TILE, F32)
    for k in range(12):
        moved = pltpu.roll(t_ref[k * 16 : k * 16 + 16, :].astype(F32), (k * 8 + 3) % 128, 1)
        packed = jnp.where(group == k, moved, packed)
    edge_ref[...] = packed.astype(BF16)
    for move in moves:
        move.wait()


def send(state, planes):
    return pl.pallas_call(
        send_kernel,
        out_shape=(
            jax.ShapeDtypeStruct((4, 4, 4) + TILE, F32),
            jax.ShapeDtypeStruct((4, 304, 128), BF16),
            jax.ShapeDtypeStruct(TILE, BF16),
        ),
        in_specs=[VMEM, VMEM],
        out_specs=(HBM, HBM, VMEM),
        scratch_shapes=[pltpu.SemaphoreType.DMA((4,)), pltpu.SemaphoreType.DMA((4,))],
        name="send",
    )(state, planes)


def merge(near, far):
    odd = axis_index("space") % 2
    return jnp.where((lane_of(near.shape) % 8 < 3) == (odd == 1), near, far)


def fill_kernel(near_ref, far_ref, c_in, c_ref, side_ref, sem):
    edge = merge(near_ref[...].astype(F32), far_ref[...].astype(F32)).astype(BF16)
    for i in range(4):
        side_ref[i] = edge
    move = pltpu.make_async_copy(side_ref, c_ref.at[:, pl.ds(288, 16)], sem)
    move.start()
    move.wait()


def in_vmem(x):
    return pltpu.with_memory_space_constraint(x, pltpu.VMEM)


def fill(near, far, copies):
    return pl.pallas_call(
        fill_kernel,
        out_shape=jax.ShapeDtypeStruct(copies.shape, BF16),
        in_specs=[VMEM, VMEM, HBM],
        out_specs=HBM,
        scratch_shapes=[pltpu.VMEM((4,) + TILE, BF16), pltpu.SemaphoreType.DMA],
        input_output_aliases={2: 0},
        name="fill",
    )(in_vmem(near), in_vmem(far), copies)


def pack_kernel(p_ref, edge_ref):
    group = lane_of(TILE) // 8
    for m in range(4):
        packed = jnp.zeros(TILE, F32)
        for g in range(16):
            moved = pltpu.roll(p_ref[m, g // 4, g % 4], (g * 8 + 3) % 128, 1)
            packed = jnp.where(group == g, moved, packed)
        edge_ref[m] = packed


def pack(states):
    return pl.pallas_call(
        pack_kernel,
        out_shape=jax.ShapeDtypeStruct((4,) + TILE, F32),
        in_specs=[VMEM],
        out_specs=VMEM,
        name="pack",
    )(in_vmem(states))


def weights_of(planes, first, last):
    a, b = planes[0], planes[1]
    aa, bb = a * a, b * b
    return [
        1.0 - aa - bb,
        0.5 * (aa - a),
        0.5 * (aa + a),
        jnp.where(last, 0.0, 0.5 * (bb - b)),
        jnp.where(first, 0.0, 0.5 * (bb + b)),
    ] + planes[2:]


def apply_stencil(w_ref, k, p, east, west):
    new = []
    for f in range(4):
        north, south = pltpu.roll(p[f], 15, 0), pltpu.roll(p[f], 1, 0)
        new.append(
            (w_ref[k, 0] * p[f] + w_ref[k, 1] * east[f])
            + (w_ref[k, 2] * west[f] + (w_ref[k, 3] * north + w_ref[k, 4] * south))
        )
    new[2] = new[2] - (w_ref[k, 5] * p[0] + w_ref[k, 6] * p[1])
    new[3] = new[3] - (w_ref[k, 7] * p[0] + w_ref[k, 8] * p[1])
    return new


def advance_kernel(p_ref, near_ref, far_ref, t_ref, out_ref, w_ref, h_ref, edge_ref):
    lane = lane_of(TILE)
    row = lax.broadcasted_iota(jnp.int32, TILE, 0)
    lane_first, lane_last = lane == 0, lane == 127
    row_first, row_last = row == 0, row == 15
    edge_ref[...] = merge(near_ref[...], far_ref[...])

    def one_level(y, carry):
        side = t_ref[y, 288:304, :].astype(F32)
        for k in range(3):
            planes = [t_ref[y, (k * 6 + q) * 16 : (k * 6 + q + 1) * 16, :].astype(F32) for q in range(6)]
            for i, weight in enumerate(weights_of(planes, row_first, row_last)):
                w_ref[k, i] = weight
            if k < 2:
                planes = [pltpu.roll(side, (125 - (k * 6 + q) * 8) % 128, 1) for q in range(6)]
                for i, weight in enumerate(weights_of(planes, row_first, row_last)):
                    h_ref[k, i] = weight
        for m in range(4):
            state = [p_ref[m, f, y] for f in range(4)]
            edge = edge_ref[m]
            halo = [pltpu.roll(edge, lax.rem(253 - (4 * f + y) * 8, 128), 1) for f in range(4)]
            for k in range(3):
                east = [pltpu.roll(v, 127, 1) for v in state]
                west = [pltpu.roll(v, 1, 1) for v in state]
                halo_east = [pltpu.roll(v, 127, 1) for v in halo]
                halo_west = [pltpu.roll(v, 1, 1) for v in halo]
                new = apply_stencil(
                    w_ref,
                    k,
                    state,
                    [jnp.where(lane_last, h, v) for v, h in zip(east, halo_east)],
                    [jnp.where(lane_first, h, v) for v, h in zip(west, halo_west)],
                )
                if k < 2:
                    halo = apply_stencil(
                        h_ref,
                        k,
                        halo,
                        [jnp.where(lane_last, v, h) for v, h in zip(east, halo_east)],
                        [jnp.where(lane_first, v, h) for v, h in zip(west, halo_west)],
                    )
                state = new
            for f in range(4):
                out_ref[m, f, y] = state[f]
        return carry

    lax.fori_loop(0, 4, one_level, 0)


def advance(states, near, far, planes):
    return pl.pallas_call(
        advance_kernel,
        out_shape=pltpu.VMEM((4, 4, 4) + TILE, F32),
        in_specs=[VMEM] * 4,
        out_specs=VMEM,
        scratch_shapes=[
            pltpu.VMEM((3, 9) + TILE, F32),
            pltpu.VMEM((2, 9) + TILE, F32),
            pltpu.VMEM((4,) + TILE, F32),
        ],
        name="advance",
    )(in_vmem(states), in_vmem(near), in_vmem(far), in_vmem(planes))


def pick_kernel(b_ref, row_ref, col_ref, out_ref, val_ref, high_ref, low_ref, sems):
    owners = row_ref.shape[0]
    moves = [pltpu.make_async_copy(b_ref.at[x], out_ref.at[:, :, x], sems.at[x]) for x in range(4)]
    for move in moves:
        move.start()
    for f in range(4):
        for half in range(2):
            block = jnp.concatenate(
                [b_ref[2 * half, f].reshape(64, 128), b_ref[2 * half + 1, f].reshape(64, 128)], axis=0
            )
            block = jnp.transpose(block)
            high = block.astype(BF16)
            low = (block - high.astype(F32)).astype(BF16)
            high_ref[f * 128 : f * 128 + 128, half * 128 : half * 128 + 128] = high
            low_ref[f * 128 : f * 128 + 128, half * 128 : half * 128 + 128] = low

    line = lax.broadcasted_iota(jnp.int32, (256, 128), 0)
    lon = lax.broadcasted_iota(jnp.int32, (128, 128), 0)

    def two_owners(i, carry):
        picks = []
        for o in range(2):
            hit = line == row_ref[pl.ds(2 * i + o, 1), :]
            picks.append(jnp.where(hit, 1.0, 0.0).astype(BF16))
        pick = jnp.concatenate(picks, axis=1)
        lines = jnp.dot(high_ref[...], pick, preferred_element_type=F32)
        lines = lines + jnp.dot(low_ref[...], pick, preferred_element_type=F32)
        for o in range(2):
            hit = lon == col_ref[pl.ds(2 * i + o, 1), :]
            for f in range(4):
                part = lines[f * 128 : f * 128 + 128, o * 128 : o * 128 + 128]
                val_ref[2 * i + o, f : f + 1, :] = jnp.sum(jnp.where(hit, part, 0.0), axis=0, keepdims=True)
        return carry

    lax.fori_loop(0, owners // 2, two_owners, 0, unroll=2)
    for move in moves:
        move.wait()


def pick(blocks, rows, cols):
    owners = rows.shape[0]
    return pl.pallas_call(
        pick_kernel,
        out_shape=(
            jax.ShapeDtypeStruct((4, 4, 4) + TILE, F32),
            jax.ShapeDtypeStruct((owners, 4, 128), F32),
        ),
        in_specs=[VMEM] * 3,
        out_specs=(HBM, VMEM),
        scratch_shapes=[
            pltpu.VMEM((512, 256), BF16),
            pltpu.VMEM((512, 256), BF16),
            pltpu.SemaphoreType.DMA((4,)),
        ],
        name="pick",
    )(in_vmem(blocks), rows, cols)


def on_device(perturbation, trajectory, site_col, site_lev, obs_counts, obs_weights):
    tiles, slots = site_col.shape[0], site_col.shape[2]
    state = perturbation.reshape((4, 4, 4) + TILE)
    local = trajectory.reshape(288, 128)
    pairs = [(i, i ^ 1) for i in range(tiles)]
    crossed = [(i, (i + 1) % tiles if i % 2 else (i - 1) % tiles) for i in range(tiles)]

    blocks, copies, edge = send(state, local)
    states = lax.all_to_all(blocks, "x", 0, 0, tiled=True)
    far = lax.ppermute(edge, "space", crossed)
    near = lax.ppermute(edge, "space", pairs)
    copies = fill(near, far, copies)
    planes = lax.all_to_all(copies, "yhi", 0, 0, tiled=True)

    late, _ = lax.optimization_barrier((states, copies))
    edge = pack(late)
    far = lax.ppermute(edge, "space", crossed)
    near = lax.ppermute(edge, "space", pairs)
    blocks = advance(states, near, far, planes)
    blocks = lax.all_to_all(blocks, "x", 0, 0, tiled=True)

    live = jnp.arange(slots, dtype=jnp.int32)[None, :] < obs_counts
    level, col = site_lev[:, 0, :], site_col[:, 0, :]
    rows = jnp.where(live, (level % 4) * 64 + (level // 4) * 16 + col // 128, -1)
    final, values = pick(blocks, rows, col % 128)
    received = lax.all_to_all(values, "space", 0, 0, tiled=True)
    summed = jnp.sum(obs_weights[0] * received, axis=1)
    return (final.reshape(perturbation.shape), summed.reshape(1, 1, tiles, slots))


def solution(mesh):
    member = ("yhi", "x")
    fine = Mesh(np.asarray(mesh.devices).reshape(mesh.shape["space"], 4, 4), ("space",) + member)
    in_specs = (
        P(member, None, None, None, "space"),
        P(None, member, None, None, "space"),
        P(None, "space", None),
        P(None, "space", None),
        P(None, "space"),
        P("space", None, None, None),
    )
    out_specs = (P(member, None, None, None, "space"), P(member, "space", None, None))
    return jax.shard_map(
        on_device, mesh=fine, in_specs=in_specs, out_specs=out_specs, check_vma=False
    )
```

```python
import functools

import jax
import jax.numpy as jnp
import numpy as np
from jax import lax
from jax.experimental import pallas as pl
from jax.experimental.pallas import tpu as pltpu
from jax.sharding import Mesh
from jax.sharding import PartitionSpec as P

F32 = jnp.float32
BF16 = jnp.bfloat16
VMEM = pl.BlockSpec(memory_space=pltpu.VMEM)
HBM = pl.BlockSpec(memory_space=pltpu.HBM)
TILE = (16, 128)


axis_index = lax.axis_index


def lane_of(shape):
    return lax.broadcasted_iota(jnp.int32, shape, len(shape) - 1)


def send_kernel(t_ref, copies_ref, edge_ref, copy_sems):
    moves = [
        pltpu.make_async_copy(t_ref, copies_ref.at[i, pl.ds(0, 288)], copy_sems.at[i]) for i in range(4)
    ]
    for move in moves:
        move.start()
    group = lane_of(TILE) // 8
    packed = jnp.zeros(TILE, F32)
    for k in range(12):
        moved = pltpu.roll(t_ref[k * 16 : k * 16 + 16, :].astype(F32), (k * 8 + 3) % 128, 1)
        packed = jnp.where(group == k, moved, packed)
    edge_ref[...] = packed.astype(BF16)
    for move in moves:
        move.wait()


def send(planes):
    return pl.pallas_call(
        send_kernel,
        out_shape=(jax.ShapeDtypeStruct((4, 304, 128), BF16), jax.ShapeDtypeStruct(TILE, BF16)),
        in_specs=[VMEM],
        out_specs=(HBM, VMEM),
        scratch_shapes=[pltpu.SemaphoreType.DMA((4,))],
        name="send",
    )(planes)


def spread_kernel(t_ref, out_ref, sems):
    moves = [pltpu.make_async_copy(t_ref, out_ref.at[i], sems.at[i]) for i in range(4)]
    for move in moves:
        move.start()
    for move in moves:
        move.wait()


def spread(planes):
    return pl.pallas_call(
        spread_kernel,
        out_shape=jax.ShapeDtypeStruct((4,) + planes.shape, BF16),
        in_specs=[VMEM],
        out_specs=HBM,
        scratch_shapes=[pltpu.SemaphoreType.DMA((4,))],
        name="spread",
    )(in_vmem(planes))


def merge(near, far):
    odd = axis_index("space") % 2
    return jnp.where((lane_of(near.shape) % 8 < 3) == (odd == 1), near, far)


def fill_kernel(near_ref, far_ref, c_in, c_ref, side_ref, sem):
    edge = merge(near_ref[...].astype(F32), far_ref[...].astype(F32)).astype(BF16)
    for i in range(4):
        side_ref[i] = edge
    move = pltpu.make_async_copy(side_ref, c_ref.at[:, pl.ds(288, 16)], sem)
    move.start()
    move.wait()


def in_vmem(x):
    return pltpu.with_memory_space_constraint(x, pltpu.VMEM)


def fill(near, far, copies):
    return pl.pallas_call(
        fill_kernel,
        out_shape=jax.ShapeDtypeStruct(copies.shape, BF16),
        in_specs=[VMEM, VMEM, HBM],
        out_specs=HBM,
        scratch_shapes=[pltpu.VMEM((4,) + TILE, BF16), pltpu.SemaphoreType.DMA],
        input_output_aliases={2: 0},
        name="fill",
    )(in_vmem(near), in_vmem(far), copies)


def pack_kernel(p_ref, edge_ref):
    group = lane_of(TILE) // 8
    for f in range(4):
        packed = jnp.zeros(TILE, F32)
        for level in range(16):
            moved = pltpu.roll(p_ref[f, level // 4, level % 4], (level * 8 + 3) % 128, 1)
            packed = jnp.where(group == level, moved, packed)
        edge_ref[f] = packed


def pack(state):
    return pl.pallas_call(
        pack_kernel,
        out_shape=jax.ShapeDtypeStruct((4,) + TILE, F32),
        in_specs=[VMEM],
        out_specs=VMEM,
        name="pack",
    )(in_vmem(state))


def weights_of(planes, first, last):
    a, b = planes[0], planes[1]
    aa, bb = a * a, b * b
    return [
        1.0 - aa - bb,
        0.5 * (aa - a),
        0.5 * (aa + a),
        jnp.where(last, 0.0, 0.5 * (bb - b)),
        jnp.where(first, 0.0, 0.5 * (bb + b)),
    ] + planes[2:]


def apply_stencil(w, p, other, lane_first, lane_last):
    new = []
    for f in range(4):
        east = pltpu.roll(jnp.where(lane_first, other[f], p[f]), 127, 1)
        west = pltpu.roll(jnp.where(lane_last, other[f], p[f]), 1, 1)
        north, south = pltpu.roll(p[f], 15, 0), pltpu.roll(p[f], 1, 0)
        new.append((w[0] * p[f] + w[1] * east) + (w[2] * west + (w[3] * north + w[4] * south)))
    new[2] = new[2] - (w[5] * p[0] + w[6] * p[1])
    new[3] = new[3] - (w[7] * p[0] + w[8] * p[1])
    return new


def advance_level(planes_of, side, state, halo):
    lane = lane_of(TILE)
    row = lax.broadcasted_iota(jnp.int32, TILE, 0)
    ends = lane == 0, lane == 127
    rims = row == 0, row == 15
    for k in range(3):
        new = apply_stencil(weights_of([planes_of(k * 6 + q) for q in range(6)], *rims), state, halo, *ends)
        if k < 2:
            planes = [pltpu.roll(side, (125 - (k * 6 + q) * 8) % 128, 1) for q in range(6)]
            halo = apply_stencil(weights_of(planes, *rims), halo, state, *ends)
        state = new
    return state


def main_kernel(p_ref, near_ref, far_ref, t_ref, row_ref, col_ref, out_ref, val_ref, edge_ref, final_ref, table_ref, sem):
    owners = row_ref.shape[0]
    edge_ref[...] = merge(near_ref[...], far_ref[...])

    def one_level(level, carry):
        y, x = level // 4, lax.rem(level, 4)
        shift = lax.rem(253 - level * 8, 128)
        state = advance_level(
            lambda i: t_ref[x, y, i * 16 : i * 16 + 16, :].astype(F32),
            t_ref[x, y, 288:304, :].astype(F32),
            [p_ref[f, y, x] for f in range(4)],
            [pltpu.roll(edge_ref[f], shift, 1) for f in range(4)],
        )
        for f in range(4):
            final_ref[f, y, x] = state[f]
        return carry

    lax.fori_loop(0, 16, one_level, 0, unroll=2)
    move = pltpu.make_async_copy(final_ref, out_ref, sem)
    move.start()

    for f in range(4):
        for half in range(2):
            block = jnp.transpose(final_ref[f, 2 * half : 2 * half + 2].reshape(128, 128))
            high = block.astype(BF16)
            low = (block - high.astype(F32)).astype(BF16)
            table_ref[f * 128 : f * 128 + 128, half * 128 : half * 128 + 128] = high
            table_ref[f * 128 : f * 128 + 128, 256 + half * 128 : 384 + half * 128] = low

    line = lax.broadcasted_iota(jnp.int32, (256, 128), 0)
    lon = lax.broadcasted_iota(jnp.int32, (128, 128), 0)

    def four_owners(i, carry):
        picks = []
        for o in range(4):
            hit = line == row_ref[pl.ds(4 * i + o, 1), :]
            picks.append(jnp.where(hit, 1.0, 0.0).astype(BF16))
        pick = jnp.concatenate(picks, axis=1)
        pick = jnp.concatenate([pick, pick], axis=0)
        lines = jnp.dot(table_ref[...], pick, preferred_element_type=F32)
        for o in range(4):
            hit = lon == col_ref[pl.ds(4 * i + o, 1), :]
            for f in range(4):
                part = lines[f * 128 : f * 128 + 128, o * 128 : o * 128 + 128]
                val_ref[4 * i + o, f : f + 1, :] = jnp.sum(jnp.where(hit, part, 0.0), axis=0, keepdims=True)
        return carry

    lax.fori_loop(0, owners // 4, four_owners, 0, unroll=2)
    move.wait()


def advance_and_pick(state, near, far, planes, rows, cols):
    owners = rows.shape[0]
    return pl.pallas_call(
        main_kernel,
        out_shape=(
            jax.ShapeDtypeStruct(state.shape, F32),
            jax.ShapeDtypeStruct((owners, 4, 128), F32),
        ),
        in_specs=[VMEM] * 6,
        out_specs=(HBM, VMEM),
        scratch_shapes=[
            pltpu.VMEM((4,) + TILE, F32),
            pltpu.VMEM(state.shape, F32),
            pltpu.VMEM((512, 512), BF16),
            pltpu.SemaphoreType.DMA,
        ],
        name="advance_and_pick",
    )(in_vmem(state), in_vmem(near), in_vmem(far), in_vmem(planes), in_vmem(rows), in_vmem(cols))


def on_device(perturbation, trajectory, site_col, site_lev, obs_counts, obs_weights):
    tiles, slots = site_col.shape[0], site_col.shape[2]
    state = perturbation.reshape((4, 4, 4) + TILE)
    local = trajectory.reshape(288, 128)
    pairs = [(i, i ^ 1) for i in range(tiles)]
    crossed = [(i, (i + 1) % tiles if i % 2 else (i - 1) % tiles) for i in range(tiles)]

    copies, edge = send(local)
    far = lax.ppermute(edge, "space", crossed)
    near = lax.ppermute(edge, "space", pairs)
    copies = fill(near, far, copies)
    planes = lax.all_to_all(copies, "yhi", 0, 0, tiled=True)

    late, _ = lax.optimization_barrier((state, copies))
    edge = pack(late)
    far = lax.ppermute(edge, "space", crossed)
    near = lax.ppermute(edge, "space", pairs)
    planes = lax.all_to_all(spread(planes), "x", 0, 0, tiled=True)

    live = jnp.arange(slots, dtype=jnp.int32)[None, :] < obs_counts
    rows = jnp.where(live, site_lev[:, 0, :] * 16 + site_col[:, 0, :] // 128, -1)
    cols = site_col[:, 0, :] % 128
    final, values = advance_and_pick(state, near, far, planes, rows, cols)
    received = lax.all_to_all(values, "space", 0, 0, tiled=True)
    summed = jnp.sum(obs_weights[0] * received, axis=1)
    return (final.reshape(perturbation.shape), summed.reshape(1, 1, tiles, slots))


def solution(mesh):
    member = ("yhi", "x")
    fine = Mesh(np.asarray(mesh.devices).reshape(mesh.shape["space"], 4, 4), ("space",) + member)
    in_specs = (
        P(member, None, None, None, "space"),
        P(None, member, None, None, "space"),
        P(None, "space", None),
        P(None, "space", None),
        P(None, "space"),
        P("space", None, None, None),
    )
    out_specs = (P(member, None, None, None, "space"), P(member, "space", None, None))
    return jax.shard_map(
        on_device, mesh=fine, in_specs=in_specs, out_specs=out_specs, check_vma=False
    )
```

```python
import functools

import jax
import jax.numpy as jnp
import numpy as np
from jax import lax
from jax.experimental import pallas as pl
from jax.experimental.pallas import tpu as pltpu
from jax.sharding import Mesh
from jax.sharding import PartitionSpec as P

F32 = jnp.float32
BF16 = jnp.bfloat16
VMEM = pl.BlockSpec(memory_space=pltpu.VMEM)
HBM = pl.BlockSpec(memory_space=pltpu.HBM)
TILE = (16, 128)


axis_index = lax.axis_index


def lane_of(shape):
    return lax.broadcasted_iota(jnp.int32, shape, len(shape) - 1)


def in_vmem(x):
    return pltpu.with_memory_space_constraint(x, pltpu.VMEM)


def spread_kernel(t_ref, out_ref, sems):
    moves = [pltpu.make_async_copy(t_ref, out_ref.at[i], sems.at[i]) for i in range(4)]
    for move in moves:
        move.start()
    for move in moves:
        move.wait()


def spread(planes):
    return pl.pallas_call(
        spread_kernel,
        out_shape=jax.ShapeDtypeStruct((4,) + planes.shape, BF16),
        in_specs=[VMEM],
        out_specs=HBM,
        scratch_shapes=[pltpu.SemaphoreType.DMA((4,))],
        name="spread",
    )(planes)


def pack_kernel(p_ref, t_ref, edge_ref):
    group = lane_of(TILE) // 8
    for f in range(4):
        packed = jnp.zeros(TILE, F32)
        for level in range(16):
            moved = pltpu.roll(p_ref[f, level // 4, level % 4], (level * 8 + 3) % 128, 1)
            packed = jnp.where(group == level, moved, packed)
        edge_ref[f] = packed
    for y in range(4):
        packed = jnp.zeros(TILE, F32)
        for k in range(12):
            moved = pltpu.roll(t_ref[y, k * 16 : k * 16 + 16, :].astype(F32), (k * 8 + 3) % 128, 1)
            packed = jnp.where(group == k, moved, packed)
        edge_ref[4 + y] = packed


def pack(state, planes):
    return pl.pallas_call(
        pack_kernel,
        out_shape=jax.ShapeDtypeStruct((8,) + TILE, F32),
        in_specs=[VMEM, VMEM],
        out_specs=VMEM,
        name="pack",
    )(in_vmem(state), in_vmem(planes))


def merge(near, far):
    odd = axis_index("space") % 2
    return jnp.where((lane_of(near.shape) % 8 < 3) == (odd == 1), near, far)


def fill_kernel(near_ref, far_ref, halo_ref, side_ref):
    edge = merge(near_ref[...], far_ref[...])
    halo_ref[...] = edge[0:4]
    for i in range(4):
        side_ref[i] = edge[4:8].astype(BF16)


def fill(near, far):
    return pl.pallas_call(
        fill_kernel,
        out_shape=(jax.ShapeDtypeStruct((4,) + TILE, F32), jax.ShapeDtypeStruct((4, 4) + TILE, BF16)),
        in_specs=[VMEM, VMEM],
        out_specs=(VMEM, VMEM),
        name="fill",
    )(in_vmem(near), in_vmem(far))


def weights_of(planes, first, last):
    a, b = planes[0], planes[1]
    aa, bb = a * a, b * b
    return [
        1.0 - aa - bb,
        0.5 * (aa - a),
        0.5 * (aa + a),
        jnp.where(last, 0.0, 0.5 * (bb - b)),
        jnp.where(first, 0.0, 0.5 * (bb + b)),
    ] + planes[2:]


def apply_stencil(w, p, other, lane_first, lane_last):
    new = []
    for f in range(4):
        east = pltpu.roll(jnp.where(lane_first, other[f], p[f]), 127, 1)
        west = pltpu.roll(jnp.where(lane_last, other[f], p[f]), 1, 1)
        north, south = pltpu.roll(p[f], 15, 0), pltpu.roll(p[f], 1, 0)
        new.append((w[0] * p[f] + w[1] * east) + (w[2] * west + (w[3] * north + w[4] * south)))
    new[2] = new[2] - (w[5] * p[0] + w[6] * p[1])
    new[3] = new[3] - (w[7] * p[0] + w[8] * p[1])
    return new


def advance_level(planes_of, side, state, halo):
    lane = lane_of(TILE)
    row = lax.broadcasted_iota(jnp.int32, TILE, 0)
    ends = lane == 0, lane == 127
    rims = row == 0, row == 15
    for k in range(3):
        new = apply_stencil(weights_of([planes_of(k * 6 + q) for q in range(6)], *rims), state, halo, *ends)
        if k < 2:
            planes = [pltpu.roll(side, (125 - (k * 6 + q) * 8) % 128, 1) for q in range(6)]
            halo = apply_stencil(weights_of(planes, *rims), halo, state, *ends)
        state = new
    return state


def advance_at(y, x, p_ref, halo_ref, planes_of, side):
    shift = lax.rem(253 - (4 * y + x) * 8, 128)
    state = [p_ref[f, y, x] for f in range(4)]
    halo = [pltpu.roll(halo_ref[f], shift, 1) for f in range(4)]
    return advance_level(planes_of, side.astype(F32), state, halo)


def own_kernel(p_ref, halo_ref, t_ref, side_ref, out_ref):
    x = axis_index("x")

    def one_level(y, carry):
        state = advance_at(
            y, x, p_ref, halo_ref, lambda i: t_ref[y, i * 16 : i * 16 + 16, :].astype(F32), side_ref[0, y]
        )
        for f in range(4):
            out_ref[f, y] = state[f]
        return carry

    lax.fori_loop(0, 4, one_level, 0, unroll=2)


def advance_own(state, halo, planes, side):
    return pl.pallas_call(
        own_kernel,
        out_shape=jax.ShapeDtypeStruct((4, 4) + TILE, F32),
        in_specs=[VMEM] * 4,
        out_specs=VMEM,
        name="advance_own",
    )(in_vmem(state), halo, in_vmem(planes), side)


def main_kernel(
    p_ref, halo_ref, own_ref, t_ref, side_ref, row_ref, col_ref, out_ref, val_ref, final_ref, table_ref, sem
):
    owners = row_ref.shape[0]
    here = axis_index("x")

    def one_level(i, carry):
        y, x = lax.rem(i, 4), lax.rem(here + 1 + i // 4, 4)
        state = advance_at(
            y, x, p_ref, halo_ref, lambda j: t_ref[x, y, j * 16 : j * 16 + 16, :].astype(F32), side_ref[x, y]
        )
        for f in range(4):
            final_ref[f, y, x] = state[f]
        return carry

    lax.fori_loop(0, 12, one_level, 0, unroll=2)
    for f in range(4):
        for y in range(4):
            final_ref[f, y, here] = own_ref[f, y]
    move = pltpu.make_async_copy(final_ref, out_ref, sem)
    move.start()

    for f in range(4):
        for half in range(2):
            block = jnp.transpose(final_ref[f, 2 * half : 2 * half + 2].reshape(128, 128))
            high = block.astype(BF16)
            low = (block - high.astype(F32)).astype(BF16)
            table_ref[f * 128 : f * 128 + 128, half * 128 : half * 128 + 128] = high
            table_ref[f * 128 : f * 128 + 128, 256 + half * 128 : 384 + half * 128] = low

    line = lax.broadcasted_iota(jnp.int32, (256, 128), 0)
    lon = lax.broadcasted_iota(jnp.int32, (128, 128), 0)

    def four_owners(i, carry):
        picks = []
        for o in range(4):
            hit = line == row_ref[pl.ds(4 * i + o, 1), :]
            picks.append(jnp.where(hit, 1.0, 0.0).astype(BF16))
        pick = jnp.concatenate(picks, axis=1)
        pick = jnp.concatenate([pick, pick], axis=0)
        lines = jnp.dot(table_ref[...], pick, preferred_element_type=F32)
        for o in range(4):
            hit = lon == col_ref[pl.ds(4 * i + o, 1), :]
            for f in range(4):
                part = lines[f * 128 : f * 128 + 128, o * 128 : o * 128 + 128]
                val_ref[4 * i + o, f : f + 1, :] = jnp.sum(jnp.where(hit, part, 0.0), axis=0, keepdims=True)
        return carry

    lax.fori_loop(0, owners // 4, four_owners, 0, unroll=2)
    move.wait()


def advance_and_pick(state, halo, own, planes, sides, rows, cols):
    owners = rows.shape[0]
    return pl.pallas_call(
        main_kernel,
        out_shape=(
            jax.ShapeDtypeStruct(state.shape, F32),
            jax.ShapeDtypeStruct((owners, 4, 128), F32),
        ),
        in_specs=[VMEM] * 7,
        out_specs=(HBM, VMEM),
        scratch_shapes=[
            pltpu.VMEM(state.shape, F32),
            pltpu.VMEM((512, 512), BF16),
            pltpu.SemaphoreType.DMA,
        ],
        name="advance_and_pick",
    )(*map(in_vmem, (state, halo, own, planes, sides, rows, cols)))


def on_device(perturbation, trajectory, site_col, site_lev, obs_counts, obs_weights):
    tiles, slots = site_col.shape[0], site_col.shape[2]
    state = perturbation.reshape((4, 4, 4) + TILE)
    local = trajectory.reshape(288, 128)
    pairs = [(i, i ^ 1) for i in range(tiles)]
    crossed = [(i, (i + 1) % tiles if i % 2 else (i - 1) % tiles) for i in range(tiles)]

    first = lax.all_to_all(spread(local), "yhi", 0, 0, tiled=True)
    copies = spread(in_vmem(first))
    planes = lax.all_to_all(copies, "x", 0, 0, tiled=True)

    late, _ = lax.optimization_barrier((first, copies))
    edge = pack(state, late)
    far = lax.ppermute(edge, "space", crossed)
    near = lax.ppermute(edge, "space", pairs)
    halo, side = fill(near, far)
    own = advance_own(state, halo, first, side)
    side, planes = lax.optimization_barrier((side, planes))
    sides = lax.all_to_all(side, "x", 0, 0, tiled=True)

    live = jnp.arange(slots, dtype=jnp.int32)[None, :] < obs_counts
    rows = jnp.where(live, site_lev[:, 0, :] * 16 + site_col[:, 0, :] // 128, -1)
    cols = site_col[:, 0, :] % 128
    final, values = advance_and_pick(state, halo, own, planes, sides, rows, cols)
    received = lax.all_to_all(values, "space", 0, 0, tiled=True)
    summed = jnp.sum(obs_weights[0] * received, axis=1)
    return (final.reshape(perturbation.shape), summed.reshape(1, 1, tiles, slots))


def solution(mesh):
    member = ("yhi", "x")
    fine = Mesh(np.asarray(mesh.devices).reshape(mesh.shape["space"], 4, 4), ("space",) + member)
    in_specs = (
        P(member, None, None, None, "space"),
        P(None, member, None, None, "space"),
        P(None, "space", None),
        P(None, "space", None),
        P(None, "space"),
        P("space", None, None, None),
    )
    out_specs = (P(member, None, None, None, "space"), P(member, "space", None, None))
    return jax.shard_map(
        on_device, mesh=fine, in_specs=in_specs, out_specs=out_specs, check_vma=False
    )
```

```python
import functools

import jax
import jax.numpy as jnp
import numpy as np
from jax import lax
from jax.experimental import pallas as pl
from jax.experimental.pallas import tpu as pltpu
from jax.sharding import Mesh
from jax.sharding import PartitionSpec as P

F32 = jnp.float32
BF16 = jnp.bfloat16
VMEM = pl.BlockSpec(memory_space=pltpu.VMEM)
HBM = pl.BlockSpec(memory_space=pltpu.HBM)
TILE = (16, 128)


axis_index = lax.axis_index


def lane_of(shape):
    return lax.broadcasted_iota(jnp.int32, shape, len(shape) - 1)


def in_vmem(x):
    return pltpu.with_memory_space_constraint(x, pltpu.VMEM)


def spread_kernel(t_ref, out_ref, sems):
    moves = [pltpu.make_async_copy(t_ref, out_ref.at[i], sems.at[i]) for i in range(4)]
    for move in moves:
        move.start()
    for move in moves:
        move.wait()


def spread(planes):
    return pl.pallas_call(
        spread_kernel,
        out_shape=jax.ShapeDtypeStruct((4,) + planes.shape, BF16),
        in_specs=[VMEM],
        out_specs=HBM,
        scratch_shapes=[pltpu.SemaphoreType.DMA((4,))],
        name="spread",
    )(planes)


def pack_kernel(p_ref, t_ref, edge_ref):
    group = lane_of(TILE) // 8
    for f in range(4):
        packed = jnp.zeros(TILE, F32)
        for level in range(16):
            moved = pltpu.roll(p_ref[f, level // 4, level % 4], (level * 8 + 3) % 128, 1)
            packed = jnp.where(group == level, moved, packed)
        edge_ref[f] = packed
    for y in range(4):
        packed = jnp.zeros(TILE, F32)
        for k in range(12):
            moved = pltpu.roll(t_ref[y, k * 16 : k * 16 + 16, :].astype(F32), (k * 8 + 3) % 128, 1)
            packed = jnp.where(group == k, moved, packed)
        edge_ref[4 + y] = packed


def pack(state, planes):
    return pl.pallas_call(
        pack_kernel,
        out_shape=jax.ShapeDtypeStruct((8,) + TILE, F32),
        in_specs=[VMEM, VMEM],
        out_specs=VMEM,
        name="pack",
    )(in_vmem(state), in_vmem(planes))


def merge(near, far):
    odd = axis_index("space") % 2
    return jnp.where((lane_of(near.shape) % 8 < 3) == (odd == 1), near, far)


def fill_kernel(near_ref, far_ref, halo_ref, side_ref):
    edge = merge(near_ref[...], far_ref[...])
    halo_ref[...] = edge[0:4]
    for i in range(4):
        side_ref[i] = edge[4:8].astype(BF16)


def fill(near, far):
    return pl.pallas_call(
        fill_kernel,
        out_shape=(jax.ShapeDtypeStruct((4,) + TILE, F32), jax.ShapeDtypeStruct((4, 4) + TILE, BF16)),
        in_specs=[VMEM, VMEM],
        out_specs=(VMEM, VMEM),
        name="fill",
    )(in_vmem(near), in_vmem(far))


def weights_of(planes, first, last):
    a, b = planes[0], planes[1]
    aa, bb = a * a, b * b
    return [
        1.0 - aa - bb,
        0.5 * (aa - a),
        0.5 * (aa + a),
        jnp.where(last, 0.0, 0.5 * (bb - b)),
        jnp.where(first, 0.0, 0.5 * (bb + b)),
    ] + planes[2:]


def apply_stencil(w, p, other, lane_first, lane_last):
    new = []
    for f in range(4):
        east = pltpu.roll(jnp.where(lane_first, other[f], p[f]), 127, 1)
        west = pltpu.roll(jnp.where(lane_last, other[f], p[f]), 1, 1)
        north, south = pltpu.roll(p[f], 15, 0), pltpu.roll(p[f], 1, 0)
        new.append((w[0] * p[f] + w[1] * east) + (w[2] * west + (w[3] * north + w[4] * south)))
    new[2] = new[2] - (w[5] * p[0] + w[6] * p[1])
    new[3] = new[3] - (w[7] * p[0] + w[8] * p[1])
    return new


def advance_level(planes_of, side, state, halo):
    lane = lane_of(TILE)
    row = lax.broadcasted_iota(jnp.int32, TILE, 0)
    ends = lane == 0, lane == 127
    rims = row == 0, row == 15
    for k in range(3):
        new = apply_stencil(weights_of([planes_of(k * 6 + q) for q in range(6)], *rims), state, halo, *ends)
        if k < 2:
            planes = [pltpu.roll(side, (125 - (k * 6 + q) * 8) % 128, 1) for q in range(6)]
            halo = apply_stencil(weights_of(planes, *rims), halo, state, *ends)
        state = new
    return state


def advance_at(y, x, p_ref, halo_ref, planes_of, side):
    shift = lax.rem(253 - (4 * y + x) * 8, 128)
    state = [p_ref[f, y, x] for f in range(4)]
    halo = [pltpu.roll(halo_ref[f], shift, 1) for f in range(4)]
    return advance_level(planes_of, side.astype(F32), state, halo)


def own_kernel(p_ref, halo_ref, t_ref, side_ref, out_ref):
    x = axis_index("x")

    def one_level(y, carry):
        state = advance_at(
            y, x, p_ref, halo_ref, lambda i: t_ref[y, i * 16 : i * 16 + 16, :].astype(F32), side_ref[0, y]
        )
        for f in range(4):
            out_ref[f, y] = state[f]
        return carry

    lax.fori_loop(0, 4, one_level, 0, unroll=2)


def advance_own(state, halo, planes, side):
    return pl.pallas_call(
        own_kernel,
        out_shape=jax.ShapeDtypeStruct((4, 4) + TILE, F32),
        in_specs=[VMEM] * 4,
        out_specs=VMEM,
        name="advance_own",
    )(in_vmem(state), halo, in_vmem(planes), side)


def main_kernel(
    p_ref, halo_ref, own_ref, t_ref, side_ref, row_ref, col_ref, out_ref, val_ref, final_ref, table_ref, sem, own_sem
):
    owners = row_ref.shape[0]
    here = axis_index("x")
    bring = pltpu.make_async_copy(own_ref, final_ref.at[:, :, here], own_sem)
    bring.start()

    def one_level(i, carry):
        y, x = lax.rem(i, 4), lax.rem(here + 1 + i // 4, 4)
        state = advance_at(
            y, x, p_ref, halo_ref, lambda j: t_ref[x, y, j * 16 : j * 16 + 16, :].astype(F32), side_ref[x, y]
        )
        for f in range(4):
            final_ref[f, y, x] = state[f]
        return carry

    lax.fori_loop(0, 12, one_level, 0, unroll=2)
    bring.wait()
    move = pltpu.make_async_copy(final_ref, out_ref, sem)
    move.start()

    for f in range(4):
        for half in range(2):
            block = jnp.transpose(final_ref[f, 2 * half : 2 * half + 2].reshape(128, 128))
            high = block.astype(BF16)
            low = (block - high.astype(F32)).astype(BF16)
            table_ref[f * 128 : f * 128 + 128, half * 128 : half * 128 + 128] = high
            table_ref[f * 128 : f * 128 + 128, 256 + half * 128 : 384 + half * 128] = low

    line = lax.broadcasted_iota(jnp.int32, (256, 128), 0)
    lon = lax.broadcasted_iota(jnp.int32, (128, 128), 0)

    def four_owners(i, carry):
        picks = []
        for o in range(4):
            hit = line == row_ref[pl.ds(4 * i + o, 1), :]
            picks.append(jnp.where(hit, 1.0, 0.0).astype(BF16))
        pick = jnp.concatenate(picks, axis=1)
        pick = jnp.concatenate([pick, pick], axis=0)
        lines = jnp.dot(table_ref[...], pick, preferred_element_type=F32)
        for o in range(4):
            hit = lon == col_ref[pl.ds(4 * i + o, 1), :]
            for f in range(4):
                part = lines[f * 128 : f * 128 + 128, o * 128 : o * 128 + 128]
                val_ref[4 * i + o, f : f + 1, :] = jnp.sum(jnp.where(hit, part, 0.0), axis=0, keepdims=True)
        return carry

    lax.fori_loop(0, owners // 4, four_owners, 0, unroll=2)
    move.wait()


def advance_and_pick(state, halo, own, planes, sides, rows, cols):
    owners = rows.shape[0]
    return pl.pallas_call(
        main_kernel,
        out_shape=(
            jax.ShapeDtypeStruct(state.shape, F32),
            jax.ShapeDtypeStruct((owners, 4, 128), F32),
        ),
        in_specs=[VMEM, VMEM, HBM] + [VMEM] * 4,
        out_specs=(HBM, VMEM),
        scratch_shapes=[
            pltpu.VMEM(state.shape, F32),
            pltpu.VMEM((512, 512), BF16),
            pltpu.SemaphoreType.DMA,
            pltpu.SemaphoreType.DMA,
        ],
        name="advance_and_pick",
    )(in_vmem(state), in_vmem(halo), own, *map(in_vmem, (planes, sides, rows, cols)))


def on_device(perturbation, trajectory, site_col, site_lev, obs_counts, obs_weights):
    tiles, slots = site_col.shape[0], site_col.shape[2]
    state = perturbation.reshape((4, 4, 4) + TILE)
    local = trajectory.reshape(288, 128)
    pairs = [(i, i ^ 1) for i in range(tiles)]
    crossed = [(i, (i + 1) % tiles if i % 2 else (i - 1) % tiles) for i in range(tiles)]

    first = lax.all_to_all(spread(local), "yhi", 0, 0, tiled=True)
    copies = spread(in_vmem(first))
    planes = lax.all_to_all(copies, "x", 0, 0, tiled=True)

    late, _ = lax.optimization_barrier((first, copies))
    edge = pack(state, late)
    far = lax.ppermute(edge, "space", crossed)
    near = lax.ppermute(edge, "space", pairs)
    halo, side = fill(near, far)
    own = advance_own(state, halo, first, side)
    side, planes, own = lax.optimization_barrier((side, planes, own))
    sides = lax.all_to_all(side, "x", 0, 0, tiled=True)

    live = jnp.arange(slots, dtype=jnp.int32)[None, :] < obs_counts
    rows = jnp.where(live, site_lev[:, 0, :] * 16 + site_col[:, 0, :] // 128, -1)
    cols = site_col[:, 0, :] % 128
    final, values = advance_and_pick(state, halo, own, planes, sides, rows, cols)
    received = lax.all_to_all(values, "space", 0, 0, tiled=True)
    summed = jnp.sum(obs_weights[0] * received, axis=1)
    return (final.reshape(perturbation.shape), summed.reshape(1, 1, tiles, slots))


def solution(mesh):
    member = ("yhi", "x")
    fine = Mesh(np.asarray(mesh.devices).reshape(mesh.shape["space"], 4, 4), ("space",) + member)
    in_specs = (
        P(member, None, None, None, "space"),
        P(None, member, None, None, "space"),
        P(None, "space", None),
        P(None, "space", None),
        P(None, "space"),
        P("space", None, None, None),
    )
    out_specs = (P(member, None, None, None, "space"), P(member, "space", None, None))
    return jax.shard_map(
        on_device, mesh=fine, in_specs=in_specs, out_specs=out_specs, check_vma=False
    )
```

```python
import functools

import jax
import jax.numpy as jnp
import numpy as np
from jax import lax
from jax.experimental import pallas as pl
from jax.experimental.pallas import tpu as pltpu
from jax.sharding import Mesh
from jax.sharding import PartitionSpec as P

F32 = jnp.float32
BF16 = jnp.bfloat16
VMEM = pl.BlockSpec(memory_space=pltpu.VMEM)
SMEM = pl.BlockSpec(memory_space=pltpu.SMEM)
HBM = pl.BlockSpec(memory_space=pltpu.HBM)
TILE = (16, 128)


axis_index = lax.axis_index


def lane_of(shape):
    return lax.broadcasted_iota(jnp.int32, shape, len(shape) - 1)


def in_vmem(x):
    return pltpu.with_memory_space_constraint(x, pltpu.VMEM)


def spread_kernel(t_ref, out_ref, sems):
    moves = [pltpu.make_async_copy(t_ref, out_ref.at[i], sems.at[i]) for i in range(4)]
    for move in moves:
        move.start()
    for move in moves:
        move.wait()


def spread(planes):
    return pl.pallas_call(
        spread_kernel,
        out_shape=jax.ShapeDtypeStruct((4,) + planes.shape, BF16),
        in_specs=[VMEM],
        out_specs=HBM,
        scratch_shapes=[pltpu.SemaphoreType.DMA((4,))],
        name="spread",
    )(planes)


def pack_kernel(p_ref, t_ref, edge_ref):
    group = lane_of(TILE) // 8
    for f in range(4):
        packed = jnp.zeros(TILE, F32)
        for level in range(16):
            moved = pltpu.roll(p_ref[f, level // 4, level % 4], (level * 8 + 3) % 128, 1)
            packed = jnp.where(group == level, moved, packed)
        edge_ref[f] = packed
    for y in range(4):
        packed = jnp.zeros(TILE, F32)
        for k in range(12):
            moved = pltpu.roll(t_ref[y, k * 16 : k * 16 + 16, :].astype(F32), (k * 8 + 3) % 128, 1)
            packed = jnp.where(group == k, moved, packed)
        edge_ref[4 + y] = packed


def pack(state, planes):
    return pl.pallas_call(
        pack_kernel,
        out_shape=jax.ShapeDtypeStruct((8,) + TILE, F32),
        in_specs=[VMEM, VMEM],
        out_specs=VMEM,
        name="pack",
    )(in_vmem(state), in_vmem(planes))


def merge(near, far):
    odd = axis_index("space") % 2
    return jnp.where((lane_of(near.shape) % 8 < 3) == (odd == 1), near, far)


def fill_kernel(far_ref, near_ref, halo_ref, side_ref):
    edge = merge(near_ref[...], far_ref[...])
    halo_ref[...] = edge[0:4]
    for i in range(4):
        side_ref[i] = edge[4:8].astype(BF16)


def fill(far, near):
    return pl.pallas_call(
        fill_kernel,
        out_shape=(jax.ShapeDtypeStruct((4,) + TILE, F32), jax.ShapeDtypeStruct((4, 4) + TILE, BF16)),
        in_specs=[VMEM, VMEM],
        out_specs=(VMEM, VMEM),
        name="fill",
    )(in_vmem(far), in_vmem(near))


def weights_of(planes, first, last):
    a, b = planes[0], planes[1]
    aa, bb = a * a, b * b
    return [
        1.0 - aa - bb,
        0.5 * (aa - a),
        0.5 * (aa + a),
        jnp.where(last, 0.0, 0.5 * (bb - b)),
        jnp.where(first, 0.0, 0.5 * (bb + b)),
    ] + planes[2:]


def apply_stencil(w, p, other, lane_first, lane_last):
    new = []
    for f in range(4):
        east = pltpu.roll(jnp.where(lane_first, other[f], p[f]), 127, 1)
        west = pltpu.roll(jnp.where(lane_last, other[f], p[f]), 1, 1)
        north, south = pltpu.roll(p[f], 15, 0), pltpu.roll(p[f], 1, 0)
        new.append((w[0] * p[f] + w[1] * east) + (w[2] * west + (w[3] * north + w[4] * south)))
    new[2] = new[2] - (w[5] * p[0] + w[6] * p[1])
    new[3] = new[3] - (w[7] * p[0] + w[8] * p[1])
    return new


def advance_level(planes_of, side, state, halo):
    lane = lane_of(TILE)
    row = lax.broadcasted_iota(jnp.int32, TILE, 0)
    ends = lane == 0, lane == 127
    rims = row == 0, row == 15
    for k in range(3):
        new = apply_stencil(weights_of([planes_of(k * 6 + q) for q in range(6)], *rims), state, halo, *ends)
        if k < 2:
            planes = [pltpu.roll(side, (125 - (k * 6 + q) * 8) % 128, 1) for q in range(6)]
            halo = apply_stencil(weights_of(planes, *rims), halo, state, *ends)
        state = new
    return state


def advance_at(y, x, p_ref, halo_ref, planes_of, side):
    shift = lax.rem(253 - (4 * y + x) * 8, 128)
    state = [p_ref[f, y, x] for f in range(4)]
    halo = [pltpu.roll(halo_ref[f], shift, 1) for f in range(4)]
    return advance_level(planes_of, side.astype(F32), state, halo)


def own_kernel(p_ref, halo_ref, t_ref, side_ref, out_ref):
    x = axis_index("x")

    def one_level(y, carry):
        state = advance_at(
            y, x, p_ref, halo_ref, lambda i: t_ref[y, i * 16 : i * 16 + 16, :].astype(F32), side_ref[0, y]
        )
        for f in range(4):
            out_ref[f, y] = state[f]
        return carry

    lax.fori_loop(0, 4, one_level, 0, unroll=2)


def advance_own(state, halo, planes, side):
    return pl.pallas_call(
        own_kernel,
        out_shape=jax.ShapeDtypeStruct((4, 4) + TILE, F32),
        in_specs=[VMEM] * 4,
        out_specs=VMEM,
        name="advance_own",
    )(in_vmem(state), halo, in_vmem(planes), side)


def main_kernel(
    p_ref, halo_ref, own_ref, t_ref, side_ref, row_ref, col_ref, count_ref, out_ref, val_ref, final_ref, table_ref, list_ref, sem, own_sem
):
    owners = row_ref.shape[0]
    here = axis_index("x")
    bring = pltpu.make_async_copy(own_ref, final_ref.at[:, :, here], own_sem)
    bring.start()

    def one_level(i, carry):
        y, x = lax.rem(i, 4), lax.rem(here + 1 + i // 4, 4)
        state = advance_at(
            y, x, p_ref, halo_ref, lambda j: t_ref[x, y, j * 16 : j * 16 + 16, :].astype(F32), side_ref[x, y]
        )
        for f in range(4):
            final_ref[f, y, x] = state[f]
        return carry

    lax.fori_loop(0, 12, one_level, 0, unroll=2)
    bring.wait()
    move = pltpu.make_async_copy(final_ref, out_ref, sem)
    move.start()

    for f in range(4):
        for half in range(2):
            block = jnp.transpose(final_ref[f, 2 * half : 2 * half + 2].reshape(128, 128))
            high = block.astype(BF16)
            low = (block - high.astype(F32)).astype(BF16)
            table_ref[f * 128 : f * 128 + 128, half * 128 : half * 128 + 128] = high
            table_ref[f * 128 : f * 128 + 128, 256 + half * 128 : 384 + half * 128] = low

    line = lax.broadcasted_iota(jnp.int32, (256, 128), 0)
    lon = lax.broadcasted_iota(jnp.int32, (128, 128), 0)
    low_lanes = lane_of((1, 128)) < 64

    def halves(ref, a, b, second):
        one, two = ref[pl.ds(a, 1), :], ref[pl.ds(b, 1), :]
        if second:
            one = pltpu.roll(one, 64, 1)
        else:
            two = pltpu.roll(two, 64, 1)
        return jnp.where(low_lanes, one, two)

    def eight_owners(owners, second):
        pairs = [(owners[2 * i], owners[2 * i + 1]) for i in range(4)]
        picks = [jnp.where(line == halves(row_ref, a, b, second), 1.0, 0.0).astype(BF16) for a, b in pairs]
        pick = jnp.concatenate(picks, axis=1)
        pick = jnp.concatenate([pick, pick], axis=0)
        lines = jnp.dot(table_ref[...], pick, preferred_element_type=F32)
        for i, (a, b) in enumerate(pairs):
            hit = lon == halves(col_ref, a, b, second)
            values = []
            for f in range(4):
                part = lines[f * 128 : f * 128 + 128, i * 128 : i * 128 + 128]
                values.append(jnp.sum(jnp.where(hit, part, 0.0), axis=0, keepdims=True))
            values = jnp.concatenate(values, axis=0)
            turned = pltpu.roll(values, 64, 1)
            if second:
                val_ref[a, :, 64:128] = turned[:, 64:128]
                val_ref[b, :, 64:128] = values[:, 64:128]
            else:
                val_ref[a, :, 0:64] = values[:, 0:64]
                val_ref[b, :, 0:64] = turned[:, 0:64]

    def note(o, found):
        list_ref[found] = o
        return found + (count_ref[o] > 64).astype(jnp.int32)

    found = lax.fori_loop(0, owners, note, 0)
    last = list_ref[jnp.maximum(found - 1, 0)]
    for i in range(7):
        list_ref[found + i] = last
    val_ref[...] = jnp.zeros(val_ref.shape, F32)
    for i in range(owners // 8):
        eight_owners([8 * i + o for o in range(8)], False)

    def second_halves(i, carry):
        eight_owners([list_ref[8 * i + o] for o in range(8)], True)
        return carry

    lax.fori_loop(0, (found + 7) // 8, second_halves, 0)
    move.wait()


def advance_and_pick(state, halo, own, planes, sides, rows, cols, counts):
    owners = rows.shape[0]
    return pl.pallas_call(
        main_kernel,
        out_shape=(
            jax.ShapeDtypeStruct(state.shape, F32),
            jax.ShapeDtypeStruct((owners, 4, 128), F32),
        ),
        in_specs=[VMEM, VMEM, HBM] + [VMEM] * 4 + [SMEM],
        out_specs=(HBM, VMEM),
        scratch_shapes=[
            pltpu.VMEM(state.shape, F32),
            pltpu.VMEM((512, 512), BF16),
            pltpu.SMEM((owners + 8,), jnp.int32),
            pltpu.SemaphoreType.DMA,
            pltpu.SemaphoreType.DMA,
        ],
        name="advance_and_pick",
    )(in_vmem(state), in_vmem(halo), own, *map(in_vmem, (planes, sides, rows, cols)), counts)


def on_device(perturbation, trajectory, site_col, site_lev, obs_counts, obs_weights):
    tiles, slots = site_col.shape[0], site_col.shape[2]
    state = perturbation.reshape((4, 4, 4) + TILE)
    local = trajectory.reshape(288, 128)
    pairs = [(i, i ^ 1) for i in range(tiles)]
    crossed = [(i, (i + 1) % tiles if i % 2 else (i - 1) % tiles) for i in range(tiles)]

    first = lax.all_to_all(spread(local), "yhi", 0, 0, tiled=True)
    copies = spread(in_vmem(first))
    planes = lax.all_to_all(copies, "x", 0, 0, tiled=True)

    late, _ = lax.optimization_barrier((first, copies))
    edge = pack(state, late)
    far = lax.ppermute(edge, "space", crossed)
    near = lax.ppermute(edge, "space", pairs)
    halo, side = fill(far, near)
    own = advance_own(state, halo, first, side)
    side, planes, own = lax.optimization_barrier((side, planes, own))
    sides = lax.all_to_all(side, "x", 0, 0, tiled=True)

    live = jnp.arange(slots, dtype=jnp.int32)[None, :] < obs_counts
    rows = jnp.where(live, site_lev[:, 0, :] * 16 + site_col[:, 0, :] // 128, -1)
    cols = site_col[:, 0, :] % 128
    final, values = advance_and_pick(state, halo, own, planes, sides, rows, cols, obs_counts[:, 0])
    received = lax.all_to_all(values, "space", 0, 0, tiled=True)
    summed = jnp.sum(obs_weights[0] * received, axis=1)
    return (final.reshape(perturbation.shape), summed.reshape(1, 1, tiles, slots))


def solution(mesh):
    member = ("yhi", "x")
    fine = Mesh(np.asarray(mesh.devices).reshape(mesh.shape["space"], 4, 4), ("space",) + member)
    in_specs = (
        P(member, None, None, None, "space"),
        P(None, member, None, None, "space"),
        P(None, "space", None),
        P(None, "space", None),
        P(None, "space"),
        P("space", None, None, None),
    )
    out_specs = (P(member, None, None, None, "space"), P(member, "space", None, None))
    return jax.shard_map(
        on_device, mesh=fine, in_specs=in_specs, out_specs=out_specs, check_vma=False
    )
```

```python
import functools

import jax
import jax.numpy as jnp
import numpy as np
from jax import lax
from jax.experimental import pallas as pl
from jax.experimental.pallas import tpu as pltpu
from jax.sharding import Mesh
from jax.sharding import PartitionSpec as P

F32 = jnp.float32
BF16 = jnp.bfloat16
VMEM = pl.BlockSpec(memory_space=pltpu.VMEM)
HBM = pl.BlockSpec(memory_space=pltpu.HBM)
TILE = (16, 128)


axis_index = lax.axis_index


def lane_of(shape):
    return lax.broadcasted_iota(jnp.int32, shape, len(shape) - 1)


def send_kernel(t_ref, copies_ref, edge_ref, copy_sems):
    moves = [
        pltpu.make_async_copy(t_ref, copies_ref.at[i, pl.ds(0, 288)], copy_sems.at[i]) for i in range(4)
    ]
    for move in moves:
        move.start()
    group = lane_of(TILE) // 8
    packed = jnp.zeros(TILE, F32)
    for k in range(12):
        moved = pltpu.roll(t_ref[k * 16 : k * 16 + 16, :].astype(F32), (k * 8 + 3) % 128, 1)
        packed = jnp.where(group == k, moved, packed)
    edge_ref[...] = packed.astype(BF16)
    for move in moves:
        move.wait()


def send(planes):
    return pl.pallas_call(
        send_kernel,
        out_shape=(jax.ShapeDtypeStruct((4, 304, 128), BF16), jax.ShapeDtypeStruct(TILE, BF16)),
        in_specs=[VMEM],
        out_specs=(HBM, VMEM),
        scratch_shapes=[pltpu.SemaphoreType.DMA((4,))],
        name="send",
    )(planes)


def spread_kernel(t_ref, out_ref, sems):
    moves = [pltpu.make_async_copy(t_ref, out_ref.at[i], sems.at[i]) for i in range(4)]
    for move in moves:
        move.start()
    for move in moves:
        move.wait()


def spread(planes):
    return pl.pallas_call(
        spread_kernel,
        out_shape=jax.ShapeDtypeStruct((4,) + planes.shape, BF16),
        in_specs=[VMEM],
        out_specs=HBM,
        scratch_shapes=[pltpu.SemaphoreType.DMA((4,))],
        name="spread",
    )(in_vmem(planes))


def merge(near, far):
    odd = axis_index("space") % 2
    return jnp.where((lane_of(near.shape) % 8 < 3) == (odd == 1), near, far)


def fill_kernel(far_ref, near_ref, c_in, c_ref, side_ref, sem):
    edge = merge(near_ref[...].astype(F32), far_ref[...].astype(F32)).astype(BF16)
    for i in range(4):
        side_ref[i] = edge
    move = pltpu.make_async_copy(side_ref, c_ref.at[:, pl.ds(288, 16)], sem)
    move.start()
    move.wait()


def in_vmem(x):
    return pltpu.with_memory_space_constraint(x, pltpu.VMEM)


def fill(far, near, copies):
    return pl.pallas_call(
        fill_kernel,
        out_shape=jax.ShapeDtypeStruct(copies.shape, BF16),
        in_specs=[VMEM, VMEM, HBM],
        out_specs=HBM,
        scratch_shapes=[pltpu.VMEM((4,) + TILE, BF16), pltpu.SemaphoreType.DMA],
        input_output_aliases={2: 0},
        name="fill",
    )(in_vmem(far), in_vmem(near), copies)


def pack_kernel(p_ref, edge_ref):
    group = lane_of(TILE) // 8
    for f in range(4):
        packed = jnp.zeros(TILE, F32)
        for level in range(16):
            moved = pltpu.roll(p_ref[f, level // 4, level % 4], (level * 8 + 3) % 128, 1)
            packed = jnp.where(group == level, moved, packed)
        edge_ref[f] = packed


def pack(state):
    return pl.pallas_call(
        pack_kernel,
        out_shape=jax.ShapeDtypeStruct((4,) + TILE, F32),
        in_specs=[VMEM],
        out_specs=VMEM,
        name="pack",
    )(in_vmem(state))


def weights_of(planes, first, last):
    a, b = planes[0], planes[1]
    aa, bb = a * a, b * b
    return [
        1.0 - aa - bb,
        0.5 * (aa - a),
        0.5 * (aa + a),
        jnp.where(last, 0.0, 0.5 * (bb - b)),
        jnp.where(first, 0.0, 0.5 * (bb + b)),
    ] + planes[2:]


def apply_stencil(w, p, other, lane_first, lane_last):
    new = []
    for f in range(4):
        east = pltpu.roll(jnp.where(lane_first, other[f], p[f]), 127, 1)
        west = pltpu.roll(jnp.where(lane_last, other[f], p[f]), 1, 1)
        north, south = pltpu.roll(p[f], 15, 0), pltpu.roll(p[f], 1, 0)
        new.append((w[0] * p[f] + w[1] * east) + (w[2] * west + (w[3] * north + w[4] * south)))
    new[2] = new[2] - (w[5] * p[0] + w[6] * p[1])
    new[3] = new[3] - (w[7] * p[0] + w[8] * p[1])
    return new


def advance_level(planes_of, side, state, halo):
    lane = lane_of(TILE)
    row = lax.broadcasted_iota(jnp.int32, TILE, 0)
    ends = lane == 0, lane == 127
    rims = row == 0, row == 15
    for k in range(3):
        new = apply_stencil(weights_of([planes_of(k * 6 + q) for q in range(6)], *rims), state, halo, *ends)
        if k < 2:
            planes = [pltpu.roll(side, (125 - (k * 6 + q) * 8) % 128, 1) for q in range(6)]
            halo = apply_stencil(weights_of(planes, *rims), halo, state, *ends)
        state = new
    return state


def advance_at(y, x, p_ref, halo_ref, planes):
    shift = lax.rem(253 - (4 * y + x) * 8, 128)
    return advance_level(
        lambda i: planes[i * 16 : i * 16 + 16, :].astype(F32),
        planes[288:304, :].astype(F32),
        [p_ref[f, y, x] for f in range(4)],
        [pltpu.roll(halo_ref[f], shift, 1) for f in range(4)],
    )


def own_kernel(far_ref, near_ref, p_ref, t_ref, out_ref, halo_ref):
    x = axis_index("x")
    halo_ref[...] = merge(near_ref[...], far_ref[...])

    def one_level(y, carry):
        state = advance_at(y, x, p_ref, halo_ref, t_ref.at[y])
        for f in range(4):
            out_ref[f, y] = state[f]
        return carry

    lax.fori_loop(0, 4, one_level, 0, unroll=2)


def advance_own(far, near, state, planes):
    return pl.pallas_call(
        own_kernel,
        out_shape=jax.ShapeDtypeStruct((4, 4) + TILE, F32),
        in_specs=[VMEM] * 4,
        out_specs=VMEM,
        scratch_shapes=[pltpu.VMEM((4,) + TILE, F32)],
        name="advance_own",
    )(in_vmem(far), in_vmem(near), in_vmem(state), in_vmem(planes))


def main_kernel(
    far_ref, near_ref, p_ref, own_ref, t_ref, row_ref, col_ref,
    out_ref, val_ref, halo_ref, final_ref, table_ref, sem, own_sem,
):
    owners = row_ref.shape[0]
    halo_ref[...] = merge(near_ref[...], far_ref[...])
    here = axis_index("x")
    bring = pltpu.make_async_copy(own_ref, final_ref.at[:, :, here], own_sem)
    bring.start()

    def one_level(i, carry):
        y, x = lax.rem(i, 4), lax.rem(here + 1 + i // 4, 4)
        state = advance_at(y, x, p_ref, halo_ref, t_ref.at[x, y])
        for f in range(4):
            final_ref[f, y, x] = state[f]
        return carry

    lax.fori_loop(0, 12, one_level, 0, unroll=2)
    bring.wait()
    move = pltpu.make_async_copy(final_ref, out_ref, sem)
    move.start()

    for f in range(4):
        for half in range(2):
            block = jnp.transpose(final_ref[f, 2 * half : 2 * half + 2].reshape(128, 128))
            high = block.astype(BF16)
            low = (block - high.astype(F32)).astype(BF16)
            table_ref[f * 128 : f * 128 + 128, half * 128 : half * 128 + 128] = high
            table_ref[f * 128 : f * 128 + 128, 256 + half * 128 : 384 + half * 128] = low

    line = lax.broadcasted_iota(jnp.int32, (256, 128), 0)
    lon = lax.broadcasted_iota(jnp.int32, (128, 128), 0)

    def four_owners(i, carry):
        picks = []
        for o in range(4):
            hit = line == row_ref[pl.ds(4 * i + o, 1), :]
            picks.append(jnp.where(hit, 1.0, 0.0).astype(BF16))
        pick = jnp.concatenate(picks, axis=1)
        pick = jnp.concatenate([pick, pick], axis=0)
        lines = jnp.dot(table_ref[...], pick, preferred_element_type=F32)
        for o in range(4):
            hit = lon == col_ref[pl.ds(4 * i + o, 1), :]
            for f in range(4):
                part = lines[f * 128 : f * 128 + 128, o * 128 : o * 128 + 128]
                val_ref[4 * i + o, f : f + 1, :] = jnp.sum(jnp.where(hit, part, 0.0), axis=0, keepdims=True)
        return carry

    lax.fori_loop(0, owners // 4, four_owners, 0, unroll=6)
    move.wait()


def advance_and_pick(far, near, state, own, planes, rows, cols):
    owners = rows.shape[0]
    return pl.pallas_call(
        main_kernel,
        out_shape=(
            jax.ShapeDtypeStruct(state.shape, F32),
            jax.ShapeDtypeStruct((owners, 4, 128), F32),
        ),
        in_specs=[VMEM, VMEM, VMEM, HBM] + [VMEM] * 3,
        out_specs=(HBM, VMEM),
        scratch_shapes=[
            pltpu.VMEM((4,) + TILE, F32),
            pltpu.VMEM(state.shape, F32),
            pltpu.VMEM((512, 512), BF16),
            pltpu.SemaphoreType.DMA,
            pltpu.SemaphoreType.DMA,
        ],
        name="advance_and_pick",
    )(in_vmem(far), in_vmem(near), in_vmem(state), own, *map(in_vmem, (planes, rows, cols)))


def on_device(perturbation, trajectory, site_col, site_lev, obs_counts, obs_weights):
    tiles, slots = site_col.shape[0], site_col.shape[2]
    state = perturbation.reshape((4, 4, 4) + TILE)
    local = trajectory.reshape(288, 128)
    pairs = [(i, i ^ 1) for i in range(tiles)]
    crossed = [(i, (i + 1) % tiles if i % 2 else (i - 1) % tiles) for i in range(tiles)]

    copies, edge = send(local)
    far = lax.ppermute(edge, "space", crossed)
    near = lax.ppermute(edge, "space", pairs)
    copies = fill(far, near, copies)
    first = lax.all_to_all(copies, "yhi", 0, 0, tiled=True)
    copies = spread(first)
    planes = lax.all_to_all(copies, "x", 0, 0, tiled=True)

    late, _ = lax.optimization_barrier((state, copies))
    edge = pack(late)
    far = lax.ppermute(edge, "space", crossed)
    near = lax.ppermute(edge, "space", pairs)
    own = advance_own(far, near, state, first)

    live = jnp.arange(slots, dtype=jnp.int32)[None, :] < obs_counts
    rows = jnp.where(live, site_lev[:, 0, :] * 16 + site_col[:, 0, :] // 128, -1)
    cols = site_col[:, 0, :] % 128
    final, values = advance_and_pick(far, near, state, own, planes, rows, cols)
    received = lax.all_to_all(values, "space", 0, 0, tiled=True)
    summed = jnp.sum(obs_weights[0] * received, axis=1)
    return (final.reshape(perturbation.shape), summed.reshape(1, 1, tiles, slots))


def solution(mesh):
    member = ("yhi", "x")
    fine = Mesh(np.asarray(mesh.devices).reshape(mesh.shape["space"], 4, 4), ("space",) + member)
    in_specs = (
        P(member, None, None, None, "space"),
        P(None, member, None, None, "space"),
        P(None, "space", None),
        P(None, "space", None),
        P(None, "space"),
        P("space", None, None, None),
    )
    out_specs = (P(member, None, None, None, "space"), P(member, "space", None, None))
    return jax.shard_map(
        on_device, mesh=fine, in_specs=in_specs, out_specs=out_specs, check_vma=False
    )
```

```python
import functools

import jax
import jax.numpy as jnp
import numpy as np
from jax import lax
from jax.experimental import pallas as pl
from jax.experimental.pallas import tpu as pltpu
from jax.sharding import Mesh
from jax.sharding import PartitionSpec as P

F32 = jnp.float32
BF16 = jnp.bfloat16
VMEM = pl.BlockSpec(memory_space=pltpu.VMEM)
HBM = pl.BlockSpec(memory_space=pltpu.HBM)
TILE = (16, 128)


axis_index = lax.axis_index


def lane_of(shape):
    return lax.broadcasted_iota(jnp.int32, shape, len(shape) - 1)


def in_vmem(x):
    return pltpu.with_memory_space_constraint(x, pltpu.VMEM)


def spread_kernel(t_ref, out_ref, sems):
    moves = [pltpu.make_async_copy(t_ref, out_ref.at[i], sems.at[i]) for i in range(4)]
    for move in moves:
        move.start()
    for move in moves:
        move.wait()


def spread(planes):
    return pl.pallas_call(
        spread_kernel,
        out_shape=jax.ShapeDtypeStruct((4,) + planes.shape, BF16),
        in_specs=[VMEM],
        out_specs=HBM,
        scratch_shapes=[pltpu.SemaphoreType.DMA((4,))],
        name="spread",
    )(planes)


def pack_kernel(p_ref, t_ref, edge_ref):
    group = lane_of(TILE) // 8
    for f in range(4):
        packed = jnp.zeros(TILE, F32)
        for level in range(16):
            moved = pltpu.roll(p_ref[f, level // 4, level % 4], (level * 8 + 3) % 128, 1)
            packed = jnp.where(group == level, moved, packed)
        edge_ref[f] = packed
    for y in range(4):
        packed = jnp.zeros(TILE, F32)
        for k in range(12):
            moved = pltpu.roll(t_ref[y, k * 16 : k * 16 + 16, :].astype(F32), (k * 8 + 3) % 128, 1)
            packed = jnp.where(group == k, moved, packed)
        edge_ref[4 + y] = packed


def pack(state, planes):
    return pl.pallas_call(
        pack_kernel,
        out_shape=jax.ShapeDtypeStruct((8,) + TILE, F32),
        in_specs=[VMEM, VMEM],
        out_specs=VMEM,
        name="pack",
    )(in_vmem(state), in_vmem(planes))


def merge(near, far):
    odd = axis_index("space") % 2
    return jnp.where((lane_of(near.shape) % 8 < 3) == (odd == 1), near, far)


def fill_kernel(far_ref, near_ref, halo_ref, side_ref):
    edge = merge(near_ref[...], far_ref[...])
    halo_ref[...] = edge[0:4]
    for i in range(4):
        side_ref[i] = edge[4:8].astype(BF16)


def fill(far, near):
    return pl.pallas_call(
        fill_kernel,
        out_shape=(jax.ShapeDtypeStruct((4,) + TILE, F32), jax.ShapeDtypeStruct((4, 4) + TILE, BF16)),
        in_specs=[VMEM, VMEM],
        out_specs=(VMEM, VMEM),
        name="fill",
    )(in_vmem(far), in_vmem(near))


def weights_of(planes, first, last):
    a, b = planes[0], planes[1]
    aa, bb = a * a, b * b
    return [
        1.0 - aa - bb,
        0.5 * (aa - a),
        0.5 * (aa + a),
        jnp.where(last, 0.0, 0.5 * (bb - b)),
        jnp.where(first, 0.0, 0.5 * (bb + b)),
    ] + planes[2:]


def apply_stencil(w, p, other, lane_first, lane_last):
    new = []
    for f in range(4):
        east = pltpu.roll(jnp.where(lane_first, other[f], p[f]), 127, 1)
        west = pltpu.roll(jnp.where(lane_last, other[f], p[f]), 1, 1)
        north, south = pltpu.roll(p[f], 15, 0), pltpu.roll(p[f], 1, 0)
        new.append((w[0] * p[f] + w[1] * east) + (w[2] * west + (w[3] * north + w[4] * south)))
    new[2] = new[2] - (w[5] * p[0] + w[6] * p[1])
    new[3] = new[3] - (w[7] * p[0] + w[8] * p[1])
    return new


def advance_level(planes_of, side, state, halo):
    lane = lane_of(TILE)
    row = lax.broadcasted_iota(jnp.int32, TILE, 0)
    ends = lane == 0, lane == 127
    rims = row == 0, row == 15
    for k in range(3):
        new = apply_stencil(weights_of([planes_of(k * 6 + q) for q in range(6)], *rims), state, halo, *ends)
        if k < 2:
            planes = [pltpu.roll(side, (125 - (k * 6 + q) * 8) % 128, 1) for q in range(6)]
            halo = apply_stencil(weights_of(planes, *rims), halo, state, *ends)
        state = new
    return state


def advance_at(y, x, p_ref, halo_ref, planes_of, side):
    shift = lax.rem(253 - (4 * y + x) * 8, 128)
    state = [p_ref[f, y, x] for f in range(4)]
    halo = [pltpu.roll(halo_ref[f], shift, 1) for f in range(4)]
    return advance_level(planes_of, side.astype(F32), state, halo)


def own_kernel(p_ref, halo_ref, t_ref, side_ref, out_ref):
    x = axis_index("x")

    def one_level(y, carry):
        state = advance_at(
            y, x, p_ref, halo_ref, lambda i: t_ref[y, i * 16 : i * 16 + 16, :].astype(F32), side_ref[0, y]
        )
        for f in range(4):
            out_ref[f, y] = state[f]
        return carry

    lax.fori_loop(0, 4, one_level, 0, unroll=2)


def advance_own(state, halo, planes, side):
    return pl.pallas_call(
        own_kernel,
        out_shape=jax.ShapeDtypeStruct((4, 4) + TILE, F32),
        in_specs=[VMEM] * 4,
        out_specs=VMEM,
        name="advance_own",
    )(in_vmem(state), halo, in_vmem(planes), side)


def main_kernel(
    p_ref, halo_ref, own_ref, t_ref, side_ref, row_ref, col_ref, out_ref, val_ref, final_ref, table_ref, sem, own_sem
):
    owners = row_ref.shape[0]
    here = axis_index("x")
    bring = pltpu.make_async_copy(own_ref, final_ref.at[:, :, here], own_sem)
    bring.start()

    def one_level(i, carry):
        y, x = lax.rem(i, 4), lax.rem(here + 1 + i // 4, 4)
        state = advance_at(
            y, x, p_ref, halo_ref, lambda j: t_ref[x, y, j * 16 : j * 16 + 16, :].astype(F32), side_ref[x, y]
        )
        for f in range(4):
            final_ref[f, y, x] = state[f]
        return carry

    lax.fori_loop(0, 12, one_level, 0, unroll=2)
    bring.wait()
    move = pltpu.make_async_copy(final_ref, out_ref, sem)
    move.start()

    for f in range(4):
        for half in range(2):
            block = jnp.transpose(final_ref[f, 2 * half : 2 * half + 2].reshape(128, 128))
            high = block.astype(BF16)
            low = (block - high.astype(F32)).astype(BF16)
            table_ref[f * 128 : f * 128 + 128, half * 128 : half * 128 + 128] = high
            table_ref[f * 128 : f * 128 + 128, 256 + half * 128 : 384 + half * 128] = low

    line = lax.broadcasted_iota(jnp.int32, (256, 128), 0)
    lon = lax.broadcasted_iota(jnp.int32, (128, 128), 0)

    def four_owners(i, carry):
        picks = []
        for o in range(4):
            hit = line == row_ref[pl.ds(4 * i + o, 1), :]
            picks.append(jnp.where(hit, 1.0, 0.0).astype(BF16))
        pick = jnp.concatenate(picks, axis=1)
        pick = jnp.concatenate([pick, pick], axis=0)
        lines = jnp.dot(table_ref[...], pick, preferred_element_type=F32)
        for o in range(4):
            hit = lon == col_ref[pl.ds(4 * i + o, 1), :]
            for f in range(4):
                part = lines[f * 128 : f * 128 + 128, o * 128 : o * 128 + 128]
                val_ref[4 * i + o, f : f + 1, :] = jnp.sum(jnp.where(hit, part, 0.0), axis=0, keepdims=True)
        return carry

    lax.fori_loop(0, owners // 4, four_owners, 0, unroll=6)
    move.wait()


def advance_and_pick(state, halo, own, planes, sides, rows, cols):
    owners = rows.shape[0]
    return pl.pallas_call(
        main_kernel,
        out_shape=(
            jax.ShapeDtypeStruct(state.shape, F32),
            jax.ShapeDtypeStruct((owners, 4, 128), F32),
        ),
        in_specs=[VMEM, VMEM, HBM] + [VMEM] * 4,
        out_specs=(HBM, VMEM),
        scratch_shapes=[
            pltpu.VMEM(state.shape, F32),
            pltpu.VMEM((512, 512), BF16),
            pltpu.SemaphoreType.DMA,
            pltpu.SemaphoreType.DMA,
        ],
        name="advance_and_pick",
    )(in_vmem(state), in_vmem(halo), own, *map(in_vmem, (planes, sides, rows, cols)))


def on_device(perturbation, trajectory, site_col, site_lev, obs_counts, obs_weights):
    tiles, slots = site_col.shape[0], site_col.shape[2]
    state = perturbation.reshape((4, 4, 4) + TILE)
    local = trajectory.reshape(288, 128)
    pairs = [(i, i ^ 1) for i in range(tiles)]
    crossed = [(i, (i + 1) % tiles if i % 2 else (i - 1) % tiles) for i in range(tiles)]

    first = lax.all_to_all(spread(local), "yhi", 0, 0, tiled=True)
    copies = spread(in_vmem(first))
    planes = lax.all_to_all(copies, "x", 0, 0, tiled=True)

    late, _ = lax.optimization_barrier((first, copies))
    edge = pack(state, late)
    far = lax.ppermute(edge, "space", crossed)
    near = lax.ppermute(edge, "space", pairs)
    halo, side = fill(far, near)
    own = advance_own(state, halo, first, side)
    side, planes, own = lax.optimization_barrier((side, planes, own))
    sides = lax.all_to_all(side, "x", 0, 0, tiled=True)

    live = jnp.arange(slots, dtype=jnp.int32)[None, :] < obs_counts
    rows = jnp.where(live, site_lev[:, 0, :] * 16 + site_col[:, 0, :] // 128, -1)
    cols = site_col[:, 0, :] % 128
    final, values = advance_and_pick(state, halo, own, planes, sides, rows, cols)
    received = lax.all_to_all(values, "space", 0, 0, tiled=True)
    summed = jnp.sum(obs_weights[0] * received, axis=1)
    return (final.reshape(perturbation.shape), summed.reshape(1, 1, tiles, slots))


def solution(mesh):
    member = ("yhi", "x")
    fine = Mesh(np.asarray(mesh.devices).reshape(mesh.shape["space"], 4, 4), ("space",) + member)
    in_specs = (
        P(member, None, None, None, "space"),
        P(None, member, None, None, "space"),
        P(None, "space", None),
        P(None, "space", None),
        P(None, "space"),
        P("space", None, None, None),
    )
    out_specs = (P(member, None, None, None, "space"), P(member, "space", None, None))
    return jax.shard_map(
        on_device, mesh=fine, in_specs=in_specs, out_specs=out_specs, check_vma=False
    )
```

```python
import functools

import jax
import jax.numpy as jnp
import numpy as np
from jax import lax
from jax.experimental import pallas as pl
from jax.experimental.pallas import tpu as pltpu
from jax.sharding import Mesh
from jax.sharding import PartitionSpec as P

F32 = jnp.float32
BF16 = jnp.bfloat16
VMEM = pl.BlockSpec(memory_space=pltpu.VMEM)
HBM = pl.BlockSpec(memory_space=pltpu.HBM)
TILE = (16, 128)


axis_index = lax.axis_index


def lane_of(shape):
    return lax.broadcasted_iota(jnp.int32, shape, len(shape) - 1)


def in_vmem(x):
    return pltpu.with_memory_space_constraint(x, pltpu.VMEM)


def spread_kernel(t_ref, out_ref, sems):
    moves = [pltpu.make_async_copy(t_ref, out_ref.at[i], sems.at[i]) for i in range(4)]
    for move in moves:
        move.start()
    for move in moves:
        move.wait()


def spread(planes):
    return pl.pallas_call(
        spread_kernel,
        out_shape=jax.ShapeDtypeStruct((4,) + planes.shape, BF16),
        in_specs=[VMEM],
        out_specs=HBM,
        scratch_shapes=[pltpu.SemaphoreType.DMA((4,))],
        name="spread",
    )(planes)


def pack_kernel(p_ref, t_ref, edge_ref):
    group = lane_of(TILE) // 8
    for f in range(4):
        packed = jnp.zeros(TILE, F32)
        for level in range(16):
            moved = pltpu.roll(p_ref[f, level // 4, level % 4], (level * 8 + 3) % 128, 1)
            packed = jnp.where(group == level, moved, packed)
        edge_ref[f] = packed
    for y in range(4):
        packed = jnp.zeros(TILE, F32)
        for k in range(12):
            moved = pltpu.roll(t_ref[y, k * 16 : k * 16 + 16, :].astype(F32), (k * 8 + 3) % 128, 1)
            packed = jnp.where(group == k, moved, packed)
        edge_ref[4 + y] = packed


def pack(state, planes):
    return pl.pallas_call(
        pack_kernel,
        out_shape=jax.ShapeDtypeStruct((8,) + TILE, F32),
        in_specs=[VMEM, VMEM],
        out_specs=VMEM,
        name="pack",
    )(in_vmem(state), in_vmem(planes))


def merge(near, far):
    odd = axis_index("space") % 2
    return jnp.where((lane_of(near.shape) % 8 < 3) == (odd == 1), near, far)


def fill_kernel(far_ref, near_ref, halo_ref, side_ref):
    edge = merge(near_ref[...], far_ref[...])
    halo_ref[...] = edge[0:4]
    side_ref[...] = edge[4:8].astype(BF16)


def fill(far, near):
    return pl.pallas_call(
        fill_kernel,
        out_shape=(jax.ShapeDtypeStruct((4,) + TILE, F32), jax.ShapeDtypeStruct((4,) + TILE, BF16)),
        in_specs=[VMEM, VMEM],
        out_specs=(VMEM, VMEM),
        name="fill",
    )(in_vmem(far), in_vmem(near))


def weights_of(planes, first, last):
    a, b = planes[0], planes[1]
    aa, bb = a * a, b * b
    return [
        1.0 - aa - bb,
        0.5 * (aa - a),
        0.5 * (aa + a),
        jnp.where(last, 0.0, 0.5 * (bb - b)),
        jnp.where(first, 0.0, 0.5 * (bb + b)),
    ] + planes[2:]


def apply_stencil(w, p, other, lane_first, lane_last):
    new = []
    for f in range(4):
        east = pltpu.roll(jnp.where(lane_first, other[f], p[f]), 127, 1)
        west = pltpu.roll(jnp.where(lane_last, other[f], p[f]), 1, 1)
        north, south = pltpu.roll(p[f], 15, 0), pltpu.roll(p[f], 1, 0)
        new.append((w[0] * p[f] + w[1] * east) + (w[2] * west + (w[3] * north + w[4] * south)))
    new[2] = new[2] - (w[5] * p[0] + w[6] * p[1])
    new[3] = new[3] - (w[7] * p[0] + w[8] * p[1])
    return new


def advance_level(planes_of, side, state, halo):
    lane = lane_of(TILE)
    row = lax.broadcasted_iota(jnp.int32, TILE, 0)
    ends = lane == 0, lane == 127
    rims = row == 0, row == 15
    for k in range(3):
        new = apply_stencil(weights_of([planes_of(k * 6 + q) for q in range(6)], *rims), state, halo, *ends)
        if k < 2:
            planes = [pltpu.roll(side, (125 - (k * 6 + q) * 8) % 128, 1) for q in range(6)]
            halo = apply_stencil(weights_of(planes, *rims), halo, state, *ends)
        state = new
    return state


def advance_at(y, x, p_ref, halo_ref, planes_of, side):
    shift = lax.rem(253 - (4 * y + x) * 8, 128)
    state = [p_ref[f, y, x] for f in range(4)]
    halo = [pltpu.roll(halo_ref[f], shift, 1) for f in range(4)]
    return advance_level(planes_of, side.astype(F32), state, halo)


def own_kernel(p_ref, halo_ref, t_ref, side_ref, out_ref):
    x = axis_index("x")

    def one_level(y, carry):
        state = advance_at(
            y, x, p_ref, halo_ref, lambda i: t_ref[y, i * 16 : i * 16 + 16, :].astype(F32), side_ref[y]
        )
        for f in range(4):
            out_ref[f, y] = state[f]
        return carry

    lax.fori_loop(0, 4, one_level, 0, unroll=2)


def advance_own(state, halo, planes, side):
    return pl.pallas_call(
        own_kernel,
        out_shape=jax.ShapeDtypeStruct((4, 4) + TILE, F32),
        in_specs=[VMEM] * 4,
        out_specs=VMEM,
        name="advance_own",
    )(in_vmem(state), halo, in_vmem(planes), side)


def main_kernel(
    p_ref, halo_ref, own_ref, t_ref, side1_ref, side2_ref, side3_ref, row_ref, col_ref,
    out_ref, val_ref, side_ref, final_ref, table_ref, sem, own_sem,
):
    owners = row_ref.shape[0]
    here = axis_index("x")
    bring = pltpu.make_async_copy(own_ref, final_ref.at[:, :, here], own_sem)
    bring.start()
    for k, ref in enumerate((side1_ref, side2_ref, side3_ref)):
        side_ref[k] = ref[...]

    def one_level(i, carry):
        y, x = lax.rem(i, 4), lax.rem(here + 1 + i // 4, 4)
        state = advance_at(
            y, x, p_ref, halo_ref, lambda j: t_ref[x, y, j * 16 : j * 16 + 16, :].astype(F32), side_ref[i // 4, y]
        )
        for f in range(4):
            final_ref[f, y, x] = state[f]
        return carry

    lax.fori_loop(0, 12, one_level, 0, unroll=2)
    bring.wait()
    move = pltpu.make_async_copy(final_ref, out_ref, sem)
    move.start()

    for f in range(4):
        for half in range(2):
            block = jnp.transpose(final_ref[f, 2 * half : 2 * half + 2].reshape(128, 128))
            high = block.astype(BF16)
            low = (block - high.astype(F32)).astype(BF16)
            table_ref[f * 128 : f * 128 + 128, half * 128 : half * 128 + 128] = high
            table_ref[f * 128 : f * 128 + 128, 256 + half * 128 : 384 + half * 128] = low

    line = lax.broadcasted_iota(jnp.int32, (256, 128), 0)
    lon = lax.broadcasted_iota(jnp.int32, (128, 128), 0)

    def four_owners(i, carry):
        picks = []
        for o in range(4):
            hit = line == row_ref[pl.ds(4 * i + o, 1), :]
            picks.append(jnp.where(hit, 1.0, 0.0).astype(BF16))
        pick = jnp.concatenate(picks, axis=1)
        pick = jnp.concatenate([pick, pick], axis=0)
        lines = jnp.dot(table_ref[...], pick, preferred_element_type=F32)
        for o in range(4):
            hit = lon == col_ref[pl.ds(4 * i + o, 1), :]
            for f in range(4):
                part = lines[f * 128 : f * 128 + 128, o * 128 : o * 128 + 128]
                val_ref[4 * i + o, f : f + 1, :] = jnp.sum(jnp.where(hit, part, 0.0), axis=0, keepdims=True)
        return carry

    lax.fori_loop(0, owners // 4, four_owners, 0, unroll=6)
    move.wait()


def advance_and_pick(state, halo, own, planes, sides, rows, cols):
    owners = rows.shape[0]
    return pl.pallas_call(
        main_kernel,
        out_shape=(
            jax.ShapeDtypeStruct(state.shape, F32),
            jax.ShapeDtypeStruct((owners, 4, 128), F32),
        ),
        in_specs=[VMEM, VMEM, HBM] + [VMEM] * 6,
        out_specs=(HBM, VMEM),
        scratch_shapes=[
            pltpu.VMEM((3, 4) + TILE, BF16),
            pltpu.VMEM(state.shape, F32),
            pltpu.VMEM((512, 512), BF16),
            pltpu.SemaphoreType.DMA,
            pltpu.SemaphoreType.DMA,
        ],
        name="advance_and_pick",
    )(in_vmem(state), in_vmem(halo), own, *map(in_vmem, (planes, *sides, rows, cols)))


def on_device(perturbation, trajectory, site_col, site_lev, obs_counts, obs_weights):
    tiles, slots = site_col.shape[0], site_col.shape[2]
    state = perturbation.reshape((4, 4, 4) + TILE)
    local = trajectory.reshape(288, 128)
    pairs = [(i, i ^ 1) for i in range(tiles)]
    crossed = [(i, (i + 1) % tiles if i % 2 else (i - 1) % tiles) for i in range(tiles)]

    first = lax.all_to_all(spread(local), "yhi", 0, 0, tiled=True)
    copies = spread(in_vmem(first))
    planes = lax.all_to_all(copies, "x", 0, 0, tiled=True)

    late, _ = lax.optimization_barrier((first, copies))
    edge = pack(state, late)
    far = lax.ppermute(edge, "space", crossed)
    near = lax.ppermute(edge, "space", pairs)
    halo, side = fill(far, near)
    own = advance_own(state, halo, first, side)
    sides = [lax.ppermute(side, "x", [((i + k) % 4, i) for i in range(4)]) for k in (1, 2, 3)]

    live = jnp.arange(slots, dtype=jnp.int32)[None, :] < obs_counts
    rows = jnp.where(live, site_lev[:, 0, :] * 16 + site_col[:, 0, :] // 128, -1)
    cols = site_col[:, 0, :] % 128
    final, values = advance_and_pick(state, halo, own, planes, sides, rows, cols)
    received = lax.all_to_all(values, "space", 0, 0, tiled=True)
    summed = jnp.sum(obs_weights[0] * received, axis=1)
    return (final.reshape(perturbation.shape), summed.reshape(1, 1, tiles, slots))


def solution(mesh):
    member = ("yhi", "x")
    fine = Mesh(np.asarray(mesh.devices).reshape(mesh.shape["space"], 4, 4), ("space",) + member)
    in_specs = (
        P(member, None, None, None, "space"),
        P(None, member, None, None, "space"),
        P(None, "space", None),
        P(None, "space", None),
        P(None, "space"),
        P("space", None, None, None),
    )
    out_specs = (P(member, None, None, None, "space"), P(member, "space", None, None))
    return jax.shard_map(
        on_device, mesh=fine, in_specs=in_specs, out_specs=out_specs, check_vma=False
    )
```

```python
import functools

import jax
import jax.numpy as jnp
import numpy as np
from jax import lax
from jax.experimental import pallas as pl
from jax.experimental.pallas import tpu as pltpu
from jax.sharding import Mesh
from jax.sharding import PartitionSpec as P

F32 = jnp.float32
BF16 = jnp.bfloat16
VMEM = pl.BlockSpec(memory_space=pltpu.VMEM)
HBM = pl.BlockSpec(memory_space=pltpu.HBM)
TILE = (16, 128)


axis_index = lax.axis_index


def lane_of(shape):
    return lax.broadcasted_iota(jnp.int32, shape, len(shape) - 1)


def in_vmem(x):
    return pltpu.with_memory_space_constraint(x, pltpu.VMEM)


def spread_kernel(t_ref, out_ref, sems):
    moves = [pltpu.make_async_copy(t_ref, out_ref.at[i], sems.at[i]) for i in range(4)]
    for move in moves:
        move.start()
    for move in moves:
        move.wait()


def spread(planes):
    return pl.pallas_call(
        spread_kernel,
        out_shape=jax.ShapeDtypeStruct((4,) + planes.shape, BF16),
        in_specs=[VMEM],
        out_specs=HBM,
        scratch_shapes=[pltpu.SemaphoreType.DMA((4,))],
        name="spread",
    )(planes)


def pack_kernel(p_ref, t_ref, edge_ref):
    group = lane_of(TILE) // 8
    for f in range(4):
        packed = jnp.zeros(TILE, F32)
        for level in range(16):
            moved = pltpu.roll(p_ref[f, level // 4, level % 4], (level * 8 + 3) % 128, 1)
            packed = jnp.where(group == level, moved, packed)
        edge_ref[f] = packed
    for y in range(4):
        packed = jnp.zeros(TILE, F32)
        for k in range(12):
            moved = pltpu.roll(t_ref[y, k * 16 : k * 16 + 16, :].astype(F32), (k * 8 + 3) % 128, 1)
            packed = jnp.where(group == k, moved, packed)
        edge_ref[4 + y] = packed


def pack(state, planes):
    return pl.pallas_call(
        pack_kernel,
        out_shape=jax.ShapeDtypeStruct((8,) + TILE, F32),
        in_specs=[VMEM, VMEM],
        out_specs=VMEM,
        name="pack",
    )(in_vmem(state), in_vmem(planes))


def merge(near, far):
    odd = axis_index("space") % 2
    return jnp.where((lane_of(near.shape) % 8 < 3) == (odd == 1), near, far)


def fill_kernel(far_ref, near_ref, halo_ref, side_ref):
    edge = merge(near_ref[...], far_ref[...])
    halo_ref[...] = edge[0:4]
    side_ref[...] = edge[4:8].astype(BF16)


def fill(far, near):
    return pl.pallas_call(
        fill_kernel,
        out_shape=(jax.ShapeDtypeStruct((4,) + TILE, F32), jax.ShapeDtypeStruct((4,) + TILE, BF16)),
        in_specs=[VMEM, VMEM],
        out_specs=(VMEM, VMEM),
        name="fill",
    )(in_vmem(far), in_vmem(near))


def weights_of(planes, first, last):
    a, b = planes[0], planes[1]
    aa, bb = a * a, b * b
    return [
        1.0 - aa - bb,
        0.5 * (aa - a),
        0.5 * (aa + a),
        jnp.where(last, 0.0, 0.5 * (bb - b)),
        jnp.where(first, 0.0, 0.5 * (bb + b)),
    ] + planes[2:]


def apply_stencil(w, p, other, lane_first, lane_last):
    new = []
    for f in range(4):
        east = pltpu.roll(jnp.where(lane_first, other[f], p[f]), 127, 1)
        west = pltpu.roll(jnp.where(lane_last, other[f], p[f]), 1, 1)
        north, south = pltpu.roll(p[f], 15, 0), pltpu.roll(p[f], 1, 0)
        new.append((w[0] * p[f] + w[1] * east) + (w[2] * west + (w[3] * north + w[4] * south)))
    new[2] = new[2] - (w[5] * p[0] + w[6] * p[1])
    new[3] = new[3] - (w[7] * p[0] + w[8] * p[1])
    return new


def advance_level(planes_of, side, state, halo):
    lane = lane_of(TILE)
    row = lax.broadcasted_iota(jnp.int32, TILE, 0)
    ends = lane == 0, lane == 127
    rims = row == 0, row == 15
    for k in range(3):
        new = apply_stencil(weights_of([planes_of(k * 6 + q) for q in range(6)], *rims), state, halo, *ends)
        if k < 2:
            planes = [pltpu.roll(side, (125 - (k * 6 + q) * 8) % 128, 1) for q in range(6)]
            halo = apply_stencil(weights_of(planes, *rims), halo, state, *ends)
        state = new
    return state


def advance_at(y, x, p_ref, halo_ref, planes_of, side):
    shift = lax.rem(253 - (4 * y + x) * 8, 128)
    state = [p_ref[f, y, x] for f in range(4)]
    halo = [pltpu.roll(halo_ref[f], shift, 1) for f in range(4)]
    return advance_level(planes_of, side.astype(F32), state, halo)


def own_kernel(p_ref, halo_ref, t_ref, side_ref, out_ref):
    x = axis_index("x")

    def one_level(y, carry):
        state = advance_at(
            y, x, p_ref, halo_ref, lambda i: t_ref[y, i * 16 : i * 16 + 16, :].astype(F32), side_ref[y]
        )
        for f in range(4):
            out_ref[f, y] = state[f]
        return carry

    lax.fori_loop(0, 4, one_level, 0, unroll=2)


def advance_own(state, halo, planes, side):
    return pl.pallas_call(
        own_kernel,
        out_shape=jax.ShapeDtypeStruct((4, 4) + TILE, F32),
        in_specs=[VMEM] * 4,
        out_specs=VMEM,
        name="advance_own",
    )(in_vmem(state), halo, in_vmem(planes), side)


def main_kernel(
    p_ref, far_ref, near_ref, own_ref, t_ref, side1_ref, side2_ref, side3_ref, row_ref, col_ref,
    out_ref, val_ref, halo_ref, side_ref, final_ref, table_ref, sem, own_sem,
):
    owners = row_ref.shape[0]
    here = axis_index("x")
    bring = pltpu.make_async_copy(own_ref, final_ref.at[:, :, here], own_sem)
    bring.start()
    for k, ref in enumerate((side1_ref, side2_ref, side3_ref)):
        side_ref[k] = ref[...]
    halo_ref[...] = merge(near_ref[0:4], far_ref[0:4])

    def one_level(i, carry):
        y, x = lax.rem(i, 4), lax.rem(here + 1 + i // 4, 4)
        state = advance_at(
            y, x, p_ref, halo_ref, lambda j: t_ref[x, y, j * 16 : j * 16 + 16, :].astype(F32), side_ref[i // 4, y]
        )
        for f in range(4):
            final_ref[f, y, x] = state[f]
        return carry

    lax.fori_loop(0, 12, one_level, 0, unroll=2)
    bring.wait()
    move = pltpu.make_async_copy(final_ref, out_ref, sem)
    move.start()

    for f in range(4):
        for half in range(2):
            block = jnp.transpose(final_ref[f, 2 * half : 2 * half + 2].reshape(128, 128))
            high = block.astype(BF16)
            low = (block - high.astype(F32)).astype(BF16)
            table_ref[f * 128 : f * 128 + 128, half * 128 : half * 128 + 128] = high
            table_ref[f * 128 : f * 128 + 128, 256 + half * 128 : 384 + half * 128] = low

    line = lax.broadcasted_iota(jnp.int32, (256, 128), 0)
    lon = lax.broadcasted_iota(jnp.int32, (128, 128), 0)

    def four_owners(i, carry):
        picks = []
        for o in range(4):
            hit = line == row_ref[pl.ds(4 * i + o, 1), :]
            picks.append(jnp.where(hit, 1.0, 0.0).astype(BF16))
        pick = jnp.concatenate(picks, axis=1)
        pick = jnp.concatenate([pick, pick], axis=0)
        lines = jnp.dot(table_ref[...], pick, preferred_element_type=F32)
        for o in range(4):
            hit = lon == col_ref[pl.ds(4 * i + o, 1), :]
            for f in range(4):
                part = lines[f * 128 : f * 128 + 128, o * 128 : o * 128 + 128]
                val_ref[4 * i + o, f : f + 1, :] = jnp.sum(jnp.where(hit, part, 0.0), axis=0, keepdims=True)
        return carry

    lax.fori_loop(0, owners // 4, four_owners, 0, unroll=6)
    move.wait()


def advance_and_pick(state, far, near, own, planes, sides, rows, cols):
    owners = rows.shape[0]
    return pl.pallas_call(
        main_kernel,
        out_shape=(
            jax.ShapeDtypeStruct(state.shape, F32),
            jax.ShapeDtypeStruct((owners, 4, 128), F32),
        ),
        in_specs=[VMEM, VMEM, VMEM, HBM] + [VMEM] * 6,
        out_specs=(HBM, VMEM),
        scratch_shapes=[
            pltpu.VMEM((4,) + TILE, F32),
            pltpu.VMEM((3, 4) + TILE, BF16),
            pltpu.VMEM(state.shape, F32),
            pltpu.VMEM((512, 512), BF16),
            pltpu.SemaphoreType.DMA,
            pltpu.SemaphoreType.DMA,
        ],
        name="advance_and_pick",
    )(in_vmem(state), in_vmem(far), in_vmem(near), own, *map(in_vmem, (planes, *sides, rows, cols)))


def on_device(perturbation, trajectory, site_col, site_lev, obs_counts, obs_weights):
    tiles, slots = site_col.shape[0], site_col.shape[2]
    state = perturbation.reshape((4, 4, 4) + TILE)
    local = trajectory.reshape(288, 128)
    pairs = [(i, i ^ 1) for i in range(tiles)]
    crossed = [(i, (i + 1) % tiles if i % 2 else (i - 1) % tiles) for i in range(tiles)]

    first = lax.all_to_all(spread(local), "yhi", 0, 0, tiled=True)
    copies = spread(in_vmem(first))
    planes = lax.all_to_all(copies, "x", 0, 0, tiled=True)

    late, _ = lax.optimization_barrier((first, copies))
    edge = pack(state, late)
    far = lax.ppermute(edge, "space", crossed)
    near = lax.ppermute(edge, "space", pairs)
    halo, side = fill(far, near)
    own = advance_own(state, halo, first, side)
    sides = [lax.ppermute(side, "x", [((i + k) % 4, i) for i in range(4)]) for k in (1, 2, 3)]

    live = jnp.arange(slots, dtype=jnp.int32)[None, :] < obs_counts
    rows = jnp.where(live, site_lev[:, 0, :] * 16 + site_col[:, 0, :] // 128, -1)
    cols = site_col[:, 0, :] % 128
    final, values = advance_and_pick(state, far, near, own, planes, sides, rows, cols)
    received = lax.all_to_all(values, "space", 0, 0, tiled=True)
    summed = jnp.sum(obs_weights[0] * received, axis=1)
    return (final.reshape(perturbation.shape), summed.reshape(1, 1, tiles, slots))


def solution(mesh):
    member = ("yhi", "x")
    fine = Mesh(np.asarray(mesh.devices).reshape(mesh.shape["space"], 4, 4), ("space",) + member)
    in_specs = (
        P(member, None, None, None, "space"),
        P(None, member, None, None, "space"),
        P(None, "space", None),
        P(None, "space", None),
        P(None, "space"),
        P("space", None, None, None),
    )
    out_specs = (P(member, None, None, None, "space"), P(member, "space", None, None))
    return jax.shard_map(
        on_device, mesh=fine, in_specs=in_specs, out_specs=out_specs, check_vma=False
    )
```

```python
import functools

import jax
import jax.numpy as jnp
import numpy as np
from jax import lax
from jax.experimental import pallas as pl
from jax.experimental.pallas import tpu as pltpu
from jax.sharding import Mesh
from jax.sharding import PartitionSpec as P

F32 = jnp.float32
BF16 = jnp.bfloat16
VMEM = pl.BlockSpec(memory_space=pltpu.VMEM)
HBM = pl.BlockSpec(memory_space=pltpu.HBM)
TILE = (16, 128)


axis_index = lax.axis_index


def lane_of(shape):
    return lax.broadcasted_iota(jnp.int32, shape, len(shape) - 1)


def in_vmem(x):
    return pltpu.with_memory_space_constraint(x, pltpu.VMEM)


def spread_kernel(t_ref, out_ref, sems):
    moves = [pltpu.make_async_copy(t_ref, out_ref.at[i], sems.at[i]) for i in range(4)]
    for move in moves:
        move.start()
    for move in moves:
        move.wait()


def spread(planes):
    return pl.pallas_call(
        spread_kernel,
        out_shape=jax.ShapeDtypeStruct((4,) + planes.shape, BF16),
        in_specs=[VMEM],
        out_specs=HBM,
        scratch_shapes=[pltpu.SemaphoreType.DMA((4,))],
        name="spread",
    )(planes)


def pack_kernel(p_ref, t_ref, edge_ref):
    group = lane_of(TILE) // 8
    for f in range(4):
        packed = jnp.zeros(TILE, F32)
        for level in range(16):
            moved = pltpu.roll(p_ref[f, level // 4, level % 4], (level * 8 + 3) % 128, 1)
            packed = jnp.where(group == level, moved, packed)
        edge_ref[f] = packed
    for y in range(4):
        packed = jnp.zeros(TILE, F32)
        for k in range(12):
            moved = pltpu.roll(t_ref[y, k * 16 : k * 16 + 16, :].astype(F32), (k * 8 + 3) % 128, 1)
            packed = jnp.where(group == k, moved, packed)
        edge_ref[4 + y] = packed


def pack(state, planes):
    return pl.pallas_call(
        pack_kernel,
        out_shape=jax.ShapeDtypeStruct((8,) + TILE, F32),
        in_specs=[VMEM, VMEM],
        out_specs=VMEM,
        name="pack",
    )(in_vmem(state), in_vmem(planes))


def merge(near, far):
    odd = axis_index("space") % 2
    return jnp.where((lane_of(near.shape) % 8 < 3) == (odd == 1), near, far)


def fill_kernel(far_ref, near_ref, halo_ref, side_ref):
    edge = merge(near_ref[...], far_ref[...])
    halo_ref[...] = edge[0:4]
    for i in range(4):
        side_ref[i] = edge[4:8].astype(BF16)


def fill(far, near):
    return pl.pallas_call(
        fill_kernel,
        out_shape=(jax.ShapeDtypeStruct((4,) + TILE, F32), jax.ShapeDtypeStruct((4, 4) + TILE, BF16)),
        in_specs=[VMEM, VMEM],
        out_specs=(VMEM, VMEM),
        name="fill",
    )(in_vmem(far), in_vmem(near))


def weights_of(planes, first, last):
    a, b = planes[0], planes[1]
    aa, bb = a * a, b * b
    return [
        1.0 - aa - bb,
        0.5 * (aa - a),
        0.5 * (aa + a),
        jnp.where(last, 0.0, 0.5 * (bb - b)),
        jnp.where(first, 0.0, 0.5 * (bb + b)),
    ] + planes[2:]


def apply_stencil(w, p, other, lane_first, lane_last):
    new = []
    for f in range(4):
        east = pltpu.roll(jnp.where(lane_first, other[f], p[f]), 127, 1)
        west = pltpu.roll(jnp.where(lane_last, other[f], p[f]), 1, 1)
        north, south = pltpu.roll(p[f], 15, 0), pltpu.roll(p[f], 1, 0)
        new.append((w[0] * p[f] + w[1] * east) + (w[2] * west + (w[3] * north + w[4] * south)))
    new[2] = new[2] - (w[5] * p[0] + w[6] * p[1])
    new[3] = new[3] - (w[7] * p[0] + w[8] * p[1])
    return new


def advance_level(planes_of, side, state, halo):
    lane = lane_of(TILE)
    row = lax.broadcasted_iota(jnp.int32, TILE, 0)
    ends = lane == 0, lane == 127
    rims = row == 0, row == 15
    for k in range(3):
        new = apply_stencil(weights_of([planes_of(k * 6 + q) for q in range(6)], *rims), state, halo, *ends)
        if k < 2:
            planes = [pltpu.roll(side, (125 - (k * 6 + q) * 8) % 128, 1) for q in range(6)]
            halo = apply_stencil(weights_of(planes, *rims), halo, state, *ends)
        state = new
    return state


def advance_at(y, x, p_ref, halo_ref, planes_of, side):
    shift = lax.rem(253 - (4 * y + x) * 8, 128)
    state = [p_ref[f, y, x] for f in range(4)]
    halo = [pltpu.roll(halo_ref[f], shift, 1) for f in range(4)]
    return advance_level(planes_of, side.astype(F32), state, halo)


def own_kernel(p_ref, halo_ref, t_ref, side_ref, out_ref):
    x = axis_index("x")

    def one_level(y, carry):
        state = advance_at(
            y, x, p_ref, halo_ref, lambda i: t_ref[y, i * 16 : i * 16 + 16, :].astype(F32), side_ref[0, y]
        )
        for f in range(4):
            out_ref[f, y] = state[f]
        return carry

    lax.fori_loop(0, 4, one_level, 0, unroll=4)


def advance_own(state, halo, planes, side):
    return pl.pallas_call(
        own_kernel,
        out_shape=jax.ShapeDtypeStruct((4, 4) + TILE, F32),
        in_specs=[VMEM] * 4,
        out_specs=VMEM,
        name="advance_own",
    )(in_vmem(state), halo, in_vmem(planes), side)


def main_kernel(
    p_ref, halo_ref, own_ref, t_ref, side_ref, row_ref, col_ref, out_ref, val_ref, final_ref, table_ref, sem, own_sem
):
    owners = row_ref.shape[0]
    here = axis_index("x")
    bring = pltpu.make_async_copy(own_ref, final_ref.at[:, :, here], own_sem)
    bring.start()

    def one_level(i, carry):
        y, x = lax.rem(i, 4), lax.rem(here + 1 + i // 4, 4)
        state = advance_at(
            y, x, p_ref, halo_ref, lambda j: t_ref[x, y, j * 16 : j * 16 + 16, :].astype(F32), side_ref[x, y]
        )
        for f in range(4):
            final_ref[f, y, x] = state[f]
        return carry

    lax.fori_loop(0, 12, one_level, 0, unroll=3)
    bring.wait()
    move = pltpu.make_async_copy(final_ref, out_ref, sem)
    move.start()

    for f in range(4):
        for half in range(2):
            block = jnp.transpose(final_ref[f, 2 * half : 2 * half + 2].reshape(128, 128))
            high = block.astype(BF16)
            low = (block - high.astype(F32)).astype(BF16)
            table_ref[f * 128 : f * 128 + 128, half * 128 : half * 128 + 128] = high
            table_ref[f * 128 : f * 128 + 128, 256 + half * 128 : 384 + half * 128] = low

    line = lax.broadcasted_iota(jnp.int32, (256, 128), 0)
    lon = lax.broadcasted_iota(jnp.int32, (128, 128), 0)

    def four_owners(i, carry):
        picks = []
        for o in range(4):
            hit = line == row_ref[pl.ds(4 * i + o, 1), :]
            picks.append(jnp.where(hit, 1.0, 0.0).astype(BF16))
        pick = jnp.concatenate(picks, axis=1)
        pick = jnp.concatenate([pick, pick], axis=0)
        lines = jnp.dot(table_ref[...], pick, preferred_element_type=F32)
        for o in range(4):
            hit = lon == col_ref[pl.ds(4 * i + o, 1), :]
            for f in range(4):
                part = lines[f * 128 : f * 128 + 128, o * 128 : o * 128 + 128]
                val_ref[4 * i + o, f : f + 1, :] = jnp.sum(jnp.where(hit, part, 0.0), axis=0, keepdims=True)
        return carry

    lax.fori_loop(0, owners // 4, four_owners, 0, unroll=6)
    move.wait()


def advance_and_pick(state, halo, own, planes, sides, rows, cols):
    owners = rows.shape[0]
    return pl.pallas_call(
        main_kernel,
        out_shape=(
            jax.ShapeDtypeStruct(state.shape, F32),
            jax.ShapeDtypeStruct((owners, 4, 128), F32),
        ),
        in_specs=[VMEM, VMEM, HBM] + [VMEM] * 4,
        out_specs=(HBM, VMEM),
        scratch_shapes=[
            pltpu.VMEM(state.shape, F32),
            pltpu.VMEM((512, 512), BF16),
            pltpu.SemaphoreType.DMA,
            pltpu.SemaphoreType.DMA,
        ],
        name="advance_and_pick",
    )(in_vmem(state), in_vmem(halo), own, *map(in_vmem, (planes, sides, rows, cols)))


def on_device(perturbation, trajectory, site_col, site_lev, obs_counts, obs_weights):
    tiles, slots = site_col.shape[0], site_col.shape[2]
    state = perturbation.reshape((4, 4, 4) + TILE)
    local = trajectory.reshape(288, 128)
    pairs = [(i, i ^ 1) for i in range(tiles)]
    crossed = [(i, (i + 1) % tiles if i % 2 else (i - 1) % tiles) for i in range(tiles)]

    first = lax.all_to_all(spread(local), "yhi", 0, 0, tiled=True)
    copies = spread(in_vmem(first))
    planes = lax.all_to_all(copies, "x", 0, 0, tiled=True)

    late, _ = lax.optimization_barrier((first, copies))
    edge = pack(state, late)
    far = lax.ppermute(edge, "space", crossed)
    near = lax.ppermute(edge, "space", pairs)
    halo, side = fill(far, near)
    own = advance_own(state, halo, first, side)
    side, planes, own = lax.optimization_barrier((side, planes, own))
    sides = lax.all_to_all(side, "x", 0, 0, tiled=True)

    live = jnp.arange(slots, dtype=jnp.int32)[None, :] < obs_counts
    rows = jnp.where(live, site_lev[:, 0, :] * 16 + site_col[:, 0, :] // 128, -1)
    cols = site_col[:, 0, :] % 128
    final, values = advance_and_pick(state, halo, own, planes, sides, rows, cols)
    received = lax.all_to_all(values, "space", 0, 0, tiled=True)
    summed = jnp.sum(obs_weights[0] * received, axis=1)
    return (final.reshape(perturbation.shape), summed.reshape(1, 1, tiles, slots))


def solution(mesh):
    member = ("yhi", "x")
    fine = Mesh(np.asarray(mesh.devices).reshape(mesh.shape["space"], 4, 4), ("space",) + member)
    in_specs = (
        P(member, None, None, None, "space"),
        P(None, member, None, None, "space"),
        P(None, "space", None),
        P(None, "space", None),
        P(None, "space"),
        P("space", None, None, None),
    )
    out_specs = (P(member, None, None, None, "space"), P(member, "space", None, None))
    return jax.shard_map(
        on_device, mesh=fine, in_specs=in_specs, out_specs=out_specs, check_vma=False
    )
```
